32 devices in a mesh: rep: 2 (over x), atom: 8 (over z, y), dir: 2 (over core).
Axes of the slice: x: 2, y: 2, z: 4, core: 2. Of those that a mesh axis runs over, the one named last changes fastest.
Arguments:
- positions: float32 [3, 16384], P(None, ('rep', 'atom')), parts along dimension 1, may hold values from -8 to 8
- queries: bfloat16 [16384, 256], P(('rep', 'atom')), parts along dimension 0, may hold values from -6 to 6
- keys: bfloat16 [16384, 256], P(('rep', 'atom')), parts along dimension 0, may hold values from -6 to 6
- values: bfloat16 [16384, 256], P(('rep', 'atom')), parts along dimension 0, may hold values from -6 to 6
- cotangent: bfloat16 [16384, 256], P(('rep', 'atom')), parts along dimension 0, may hold values from -6 to 6
- block_counts: int32 [16], P(('rep', 'atom')), parts along dimension 0, may hold values from 1 to 1024, 6144 in all
- dir_cos: float32 [86], P('dir'), may hold values from -1 to 1
- dir_phase: float32 [86], P('dir'), may hold values from -3.140625 to 3.140625
- dir_weight: float32 [86], P('dir'), may hold values from 0.01 to 0.1
- frequencies: float32 [128], replicated, may hold values from 0.05 to 1
Outputs:
- grad_queries: bfloat16 [16384, 256], P(('rep', 'atom')), parts along dimension 0
- grad_keys: bfloat16 [16384, 256], P(('rep', 'atom')), parts along dimension 0
- grad_values: bfloat16 [16384, 256], P(('rep', 'atom')), parts along dimension 0
The draws below stay inside these ranges and needn't reach their ends.
There are 2 independent parts, one for each index of `rep`. The reference program is written for one: setup_inputs(seed, part) draws one part's arguments, and reference() takes and returns one part's arrays. A program takes and returns all parts, laid end to end along the dimension named above; an argument that names none is the same for every part. Nothing has to cross between parts.
Inputs may be any that keep to these rules, and one draw needn't show every extreme that they name: `block_counts`: atom slots of a block past its count are padding; the counts of all blocks sum to 6144.
All inputs are finite; a program needn't handle non-finite values.
Results may differ from the reference program's by a relative error of at most 0.0034.
Values may be sent and summed in bfloat16 or wider, within the bound.
No kernel may reach another device: no remote copies, remote signals or barrier semaphores. Data moves between devices by JAX's collectives and lax.ppermute only.
A program may use at most 192 MiB of HBM per device.

```python
import math
import jax
import jax.numpy as jnp
import numpy as np
from jax import lax

HEADS = 4
HD = 64
NDIR = 86
ATOM_DEV = 1024
ATOMS = 8192
BLOCKS = 8
PAIRS = 128
N_ATOM = 8


def block_levels(rng, dims, shards, low, largest):
    loudness = 1.0
    for axis_at, shards_of in shards:
        draws = jax.random.uniform(jax.random.fold_in(jax.random.fold_in(rng, 6), axis_at), (shards_of,), jnp.float32, low / len(shards), largest / len(shards))
        loudness = loudness * jnp.repeat(jnp.exp(draws), dims[axis_at] // shards_of).reshape((-1,) + (1,) * (len(dims) - 1 - axis_at))
    return loudness


def profile(number_of, total, bound, slope):
    portions = [(1 << 20) // math.isqrt(grade ** slope) + 1 for grade in range(2, number_of + 1)]
    spare, holding = total - bound - (number_of - 1), [1] * (number_of - 1)
    while spare > 0:
        free = [i for i in range(number_of - 1) if holding[i] < bound]
        mass, left = sum([portions[i] for i in free]), spare
        for i in free:
            addition = min(bound - holding[i], max(1, left * portions[i] // mass), spare)
            holding[i] = holding[i] + addition
            spare = spare - addition
    return np.array([bound] + holding)


def uneven(rng, count, total, reach, lean):
    if count == 2:
        one = jax.random.randint(rng, (), max(1, total - reach), min(reach, total - 1) + 1)
        return jnp.stack([one, total - one])
    lengths = jnp.asarray(profile(count, total, reach, lean), jnp.int32)
    couples = (count - 1) // 2
    giver, sink = lengths[1:1 + 2 * couples:2], lengths[2:2 + 2 * couples:2]
    room = jnp.minimum(giver - 1, reach - sink)
    moved = jax.random.randint(jax.random.fold_in(rng, 1), (couples,), 0, 1 << 20) % (room + 1)
    lengths = lengths.at[1:1 + 2 * couples:2].set(giver - moved).at[2:2 + 2 * couples:2].set(sink + moved)
    return lengths[jax.random.permutation(jax.random.fold_in(rng, 2), count)]


def centred(rng, shape, deviation, reach, cuts=(), held_as=jnp.bfloat16):
    entries = jax.random.normal(rng, shape, jnp.float32) * deviation
    if len(cuts) > 0:
        entries = block_levels(rng, shape, cuts, -0.22, 0.18) * entries
    return jnp.clip(entries, min=-reach, max=reach).astype(held_as)


def setup_inputs(seed: int = 0, part: int = 0) -> dict:
    splits = jax.random.split(jax.random.key(seed), 11)
    part_splits = jax.random.split(jax.random.fold_in(splits[10], part), 11)
    positions = jnp.clip(jax.random.uniform(part_splits[0], (3, ATOMS), jnp.float32, -8.0, 8.0) * block_levels(part_splits[0], (3, ATOMS), ((1, 8),), -0.4, 0.0), -8.0, 8.0)
    queries = centred(part_splits[1], (ATOMS, HEADS * HD), 1.0, 6.0, ((0, 8),))
    keys = centred(part_splits[2], (ATOMS, HEADS * HD), 1.0, 6.0, ((0, 8),))
    values = centred(part_splits[3], (ATOMS, HEADS * HD), 1.0, 6.0, ((0, 8),))
    cotangent = centred(part_splits[4], (ATOMS, HEADS * HD), 1.0, 6.0, ((0, 8),))
    block_counts = uneven(part_splits[5], BLOCKS, 3 * ATOM_DEV * N_ATOM // 4, ATOM_DEV, 2).astype(jnp.int32)
    dir_cos = jnp.clip(jax.random.uniform(splits[6], (NDIR,), jnp.float32, -1.0, 1.0) * block_levels(splits[6], (NDIR,), ((0, 2),), -0.4, 0.0), -1.0, 1.0)
    dir_phase = jnp.clip(jax.random.uniform(splits[7], (NDIR,), jnp.float32, -3.140625, 3.140625), -3.140625, 3.140625)
    dir_weight = jnp.clip(jnp.exp(math.log(0.1) - 2.3025851 * jax.random.uniform(splits[8], (NDIR,), jnp.float32) ** block_levels(splits[8], (NDIR,), ((0, 2),), -0.2, 0.2)), 0.01, 0.1)
    frequencies = jnp.clip(jnp.exp(jax.random.uniform(splits[9], (PAIRS,), jnp.float32, math.log(0.05), math.log(1.0))), 0.05, 1.0)
    return dict(positions=positions, queries=queries, keys=keys, values=values, cotangent=cotangent, block_counts=block_counts, dir_cos=dir_cos, dir_phase=dir_phase, dir_weight=dir_weight, frequencies=frequencies)


def rotate(first, second, cosine, sine):
    return (first * cosine - second * sine, first * sine + second * cosine)

def unrotate(first, second, cosine, sine):
    return (first * cosine + second * sine, second * cosine - first * sine)

def reference(positions, queries, keys, values, cotangent, block_counts, dir_cos, dir_phase, dir_weight, frequencies):
    half = HD // 2
    index = jnp.arange(ATOMS, dtype=jnp.int32)
    counts = block_counts[index // ATOM_DEV]
    mask = (index % ATOM_DEV < counts).astype(jnp.float32)
    scale = 1.0 / (8.0 * math.sqrt(ATOMS))
    sin_polar = jnp.sqrt(1.0 - dir_cos * dir_cos)
    directions = jnp.stack([sin_polar * jnp.cos(dir_phase), sin_polar * jnp.sin(dir_phase), dir_cos], axis=1)
    freq = frequencies.reshape(HEADS, half)
    q_four = queries.astype(jnp.float32).reshape(ATOMS, HEADS, 2, half) * mask[:, None, None, None]
    k_four = keys.astype(jnp.float32).reshape(ATOMS, HEADS, 2, half) * mask[:, None, None, None]
    v_three = values.astype(jnp.float32).reshape(ATOMS, HEADS, HD)
    d_three = cotangent.astype(jnp.float32).reshape(ATOMS, HEADS, HD)

    def step(carry, item):
        grad_q, grad_k, grad_v = carry
        direction, weight = item
        proj = lax.optimization_barrier(jnp.sum(positions * direction[:, None], axis=0))
        theta = proj[:, None, None] * freq[None]
        cosine = jnp.cos(theta)
        sine = jnp.sin(theta)
        qa, qb = rotate(q_four[:, :, 0], q_four[:, :, 1], cosine, sine)
        ka, kb = rotate(k_four[:, :, 0], k_four[:, :, 1], cosine, sine)
        qrot = jnp.concatenate([qa, qb], axis=2).astype(jnp.bfloat16).astype(jnp.float32)
        krot = jnp.concatenate([ka, kb], axis=2).astype(jnp.bfloat16).astype(jnp.float32)
        factor = scale * weight
        summary = jnp.einsum('ahc,ahd->hcd', factor * krot, v_three).astype(jnp.bfloat16).astype(jnp.float32)
        grad_summary = jnp.einsum('ahc,ahd->hcd', factor * qrot, d_three).astype(jnp.bfloat16).astype(jnp.float32)
        dq_rot = jnp.einsum('ahd,hcd->ahc', d_three, summary)
        dk_rot = jnp.einsum('ahd,hcd->ahc', v_three, grad_summary)
        qa2, qb2 = unrotate(dq_rot[:, :, :half], dq_rot[:, :, half:], cosine, sine)
        ka2, kb2 = unrotate(dk_rot[:, :, :half], dk_rot[:, :, half:], cosine, sine)
        grad_q = grad_q + jnp.concatenate([qa2, qb2], axis=2)
        grad_k = grad_k + jnp.concatenate([ka2, kb2], axis=2)
        grad_v = grad_v + jnp.einsum('ahc,hcd->ahd', krot, grad_summary)
        return ((grad_q, grad_k, grad_v), None)
    zeros = jnp.zeros((ATOMS, HEADS, HD), jnp.float32)
    (grad_q, grad_k, grad_v), unused = lax.scan(step, (zeros, zeros, zeros), (directions, dir_weight))
    outs = []
    for grad in (grad_q, grad_k, grad_v):
        outs.append((grad.reshape(ATOMS, HEADS * HD) * mask[:, None]).astype(jnp.bfloat16))
    return (outs[0], outs[1], outs[2])
```

```python
import functools
import math

import jax
import jax.numpy as jnp
import numpy as np
from jax import lax
from jax.experimental import pallas as pl
from jax.experimental.pallas import tpu as pltpu
from jax.sharding import PartitionSpec as P

HEADS = 4
HD = 64
HALF = 32
GROUP = 4
NODES = 16
SHARDS = 8
CHUNKS = (2, 3, 3, 3)
F32 = jnp.float32
BF16 = jnp.bfloat16
F16 = jnp.float16

_NODE = np.cos((np.arange(NODES) + 0.5) * np.pi / (2 * NODES)).astype(np.float32)


def _fit(func, terms):
    z = 0.125 * (1 - np.cos((np.arange(256) + 0.5) * np.pi / 256))
    cheb = np.polynomial.chebyshev.Chebyshev.fit(z, func(z), terms - 1, domain=[0, 0.25])
    return [float(c) for c in cheb.convert(kind=np.polynomial.Polynomial).coef]


_SIN = _fit(lambda z: np.sin(2 * np.pi * np.sqrt(z)) / np.sqrt(z), 7)
_COS = _fit(lambda z: np.cos(2 * np.pi * np.sqrt(z)), 7)


def horner(coef, z):
    acc = coef[-1] * z + coef[-2]
    for c in coef[-3::-1]:
        acc = acc * z + c
    return acc


def pair_coefs(frequencies):
    node = jnp.asarray(_NODE)
    n64 = _NODE.astype(np.float64)
    den = n64[:, None] ** 2 - n64[None, :] ** 2
    np.fill_diagonal(den, 1.0)
    inv = jnp.asarray((1.0 / den).astype(np.float32))
    f = frequencies[:, None]
    num = (f - node) * (f + node)
    fac = jnp.where(jnp.eye(NODES, dtype=bool)[None], 1.0, num[:, None, :] * inv[None])
    cosine = jnp.prod(fac, axis=2)
    sine = cosine * (f / node)
    zero = jnp.zeros_like(cosine)
    full = jnp.concatenate(
        [jnp.concatenate([cosine, zero], 1), jnp.concatenate([zero, sine], 1)], 0
    )
    one = lax.reduce_precision(full, 8, 7)
    two = lax.reduce_precision(full - one, 8, 7)
    three = full - one - two
    return jnp.concatenate([one, two, three, one, two, one], 1).astype(BF16)


def store_features(feat_ref, node_ref, proj_row):
    turns = node_ref[...] * proj_row
    turns = turns - jnp.round(turns)
    z = turns * turns
    full = jnp.concatenate([horner(_COS, z), turns * horner(_SIN, z)], axis=0)
    one = full.astype(BF16)
    rest = full - one.astype(F32)
    two = rest.astype(BF16)
    three = (rest - two.astype(F32)).astype(BF16)
    feat_ref[...] = jnp.concatenate([one, one, one, two, two, three], axis=0)


def pass_one(rows, tile, proj_ref, node_ref, coef_ref, qt_ref, kt_ref, w_ref, out_ref, feat_ref, rot_ref):
    for u in range(GROUP):
        store_features(feat_ref, node_ref, proj_ref[0, u : u + 1, :])
        lo = slice(u * HD, u * HD + HALF)
        hi = slice(u * HD + HALF, (u + 1) * HD)
        for t in range(rows // tile):
            at = slice(t * tile, (t + 1) * tile)
            trig = jnp.dot(coef_ref[...], feat_ref[:, at], preferred_element_type=F32)
            for h in range(HEADS):
                c = trig[h * HALF : (h + 1) * HALF]
                s = trig[128 + h * HALF : 128 + (h + 1) * HALF]
                for i, src in enumerate((kt_ref, qt_ref)):
                    to = slice(i * rows + t * tile, i * rows + (t + 1) * tile)
                    a = src[h * HD : h * HD + HALF, at]
                    b = src[h * HD + HALF : (h + 1) * HD, at]
                    rot_ref[h, lo, to] = (a * c - b * s).astype(BF16)
                    rot_ref[h, hi, to] = (a * s + b * c).astype(BF16)
    for h in range(HEADS):
        res = jnp.dot(rot_ref[h], w_ref[h], preferred_element_type=F32)
        for u in range(GROUP):
            out_ref[2 * h, u] = res[u * HD : u * HD + HALF]
            out_ref[2 * h + 1, u] = res[u * HD + HALF : (u + 1) * HD]


def pass_two(rows, tile, first_ref, proj_ref, node_ref, coef_ref, kt_ref, rhs_ref, sg_ref, q_in, k_in, v_in, gq_ref, gk_ref, gv_ref, feat_ref, rot_ref, d_ref):
    @pl.when(pl.program_id(0) == 0)
    def _():
        gq_ref[...] = q_in[...]
        gk_ref[...] = k_in[...]
        gv_ref[...] = v_in[...]

    for u in range(GROUP):
        store_features(feat_ref.at[u], node_ref, proj_ref[0, u : u + 1, :])
    gs = []
    for h in range(HEADS):
        parts = []
        for u in range(GROUP):
            parts.append(sg_ref[lax.rem(2 * h + first_ref[0], SHARDS), u])
            parts.append(sg_ref[lax.rem(2 * h + 1 + first_ref[0], SHARDS), u])
        sg = jnp.concatenate(parts, axis=0)
        d_ref[h] = jnp.dot(sg, rhs_ref[h], preferred_element_type=F32)
        gs.append(jnp.transpose(sg[:, HD:].astype(F32)).astype(BF16))
    for t in range(rows // tile):
        at = slice(t * tile, (t + 1) * tile)
        at2 = slice(rows + t * tile, rows + (t + 1) * tile)
        for u in range(GROUP):
            trig = jnp.dot(coef_ref[...], feat_ref[u, :, at], preferred_element_type=F32)
            ulo = slice(u * HD, u * HD + HALF)
            uhi = slice(u * HD + HALF, (u + 1) * HD)
            for h in range(HEADS):
                c = trig[h * HALF : (h + 1) * HALF]
                s = trig[128 + h * HALF : 128 + (h + 1) * HALF]
                lo = slice(h * HD, h * HD + HALF)
                hi = slice(h * HD + HALF, (h + 1) * HD)
                a = kt_ref[lo, at]
                b = kt_ref[hi, at]
                rot_ref[h, ulo, at] = (a * c - b * s).astype(BF16)
                rot_ref[h, uhi, at] = (a * s + b * c).astype(BF16)
                a = d_ref[h, ulo, at]
                b = d_ref[h, uhi, at]
                gq_ref[lo, at] += a * c + b * s
                gq_ref[hi, at] += b * c - a * s
                a = d_ref[h, ulo, at2]
                b = d_ref[h, uhi, at2]
                gk_ref[lo, at] += a * c + b * s
                gk_ref[hi, at] += b * c - a * s
    for h in range(HEADS):
        gv_ref[h * HD : (h + 1) * HD, :] += jnp.dot(gs[h], rot_ref[h], preferred_element_type=F32)


def whole(shape):
    return pl.BlockSpec(shape, lambda g: (0,) * len(shape))


def call_one(proj, node, coef, qt, kt, w, tile=256):
    steps, unused, rows = proj.shape
    nd = steps * GROUP
    return pl.pallas_call(
        functools.partial(pass_one, rows, tile),
        name="pass_one",
        grid=(steps,),
        in_specs=[
            pl.BlockSpec((1, GROUP, rows), lambda g: (g, 0, 0)),
            whole(node.shape),
            whole(coef.shape),
            whole(qt.shape),
            whole(kt.shape),
            whole(w.shape),
        ],
        out_specs=pl.BlockSpec((SHARDS, GROUP, HALF, 128), lambda g: (0, g, 0, 0)),
        out_shape=jax.ShapeDtypeStruct((SHARDS, nd, HALF, 128), F32),
        scratch_shapes=[
            pltpu.VMEM((192, rows), BF16),
            pltpu.VMEM((HEADS, GROUP * HD, 2 * rows), BF16),
        ],
        compiler_params=pltpu.CompilerParams(vmem_limit_bytes=56 << 20),
    )(proj, node, coef, qt, kt, w)


def call_two(first, proj, node, coef, kt, rhs, sg, grads, tile=128):
    steps, unused, rows = proj.shape
    width = HEADS * HD
    out = jax.ShapeDtypeStruct((width, rows), F32)
    return pl.pallas_call(
        functools.partial(pass_two, rows, tile),
        name="pass_two",
        grid=(steps,),
        in_specs=[
            pl.BlockSpec(memory_space=pltpu.SMEM),
            pl.BlockSpec((1, GROUP, rows), lambda g: (g, 0, 0)),
            whole(node.shape),
            whole(coef.shape),
            whole(kt.shape),
            whole(rhs.shape),
            pl.BlockSpec((SHARDS, GROUP, HALF, 128), lambda g: (0, g, 0, 0)),
        ]
        + [whole((width, rows))] * 3,
        out_specs=[whole((width, rows))] * 3,
        out_shape=[out] * 3,
        scratch_shapes=[
            pltpu.VMEM((GROUP, 192, rows), BF16),
            pltpu.VMEM((HEADS, GROUP * HD, rows), BF16),
            pltpu.VMEM((HEADS, GROUP * HD, 2 * rows), F32),
        ],
        input_output_aliases={7: 0, 8: 1, 9: 2},
        compiler_params=pltpu.CompilerParams(vmem_limit_bytes=60 << 20),
    )(first, proj, node, coef, kt, rhs, sg, *grads)


RING = (0, 2, 4, 6, 7, 5, 3, 1)


class Ring:
    def __init__(self, axis, count):
        self.axis = axis
        self.count = count
        where = np.argsort(np.array(RING)).astype(np.int32)
        self.me = jnp.asarray(where)[lax.axis_index(axis)]
        self.up_pairs = [(RING[i], RING[(i + 1) % count]) for i in range(count)]
        self.down_pairs = [(b, a) for a, b in self.up_pairs]

    def up(self, x):
        return lax.ppermute(x, self.axis, self.up_pairs)

    def down(self, x):
        return lax.ppermute(x, self.axis, self.down_pairs)

    def at(self, x, ahead):
        index = lax.rem(self.me + (ahead + self.count), self.count)
        return lax.dynamic_index_in_dim(x, index, 0, keepdims=False)

    def scatter_sum(self, x, gain):
        half = x.shape[1] // 2
        own = lambda d: self.at(x, d) * gain
        last = None
        for step in range(1, 5):
            ahead = 5 - step
            up, down = own(ahead), own(-ahead)
            if step == 1:
                up, down = up[:half], down[half:]
            elif step == 2:
                up = jnp.concatenate([up[:half] + last[0], up[half:]], 0)
                down = jnp.concatenate([down[:half], down[half:] + last[1]], 0)
            else:
                up, down = up + last[0], down + last[1]
            got = self.up(up.astype(F16)), self.down(down.astype(F16))
            last = [g.astype(F32) for g in got]
        return own(0) + last[0] + last[1]

    def gather(self, x):
        half = x.shape[0] // 2
        up, down = x, x
        below, above = [], []
        for step in range(3):
            up, down = self.up(up), self.down(down)
            below.append(up)
            above.append(down)
        far = jnp.concatenate([self.up(up[:half]), self.down(down[half:])], 0)
        return jnp.stack([far] + below[::-1] + [x] + above, 0)


def body(
    positions,
    queries,
    keys,
    values,
    cotangent,
    block_counts,
    dir_cos,
    dir_phase,
    dir_weight,
    frequencies,
):
    rows, width = queries.shape
    n_atom = lax.axis_size("atom")
    scale = 1.0 / (8.0 * math.sqrt(rows * n_atom))
    local = dir_cos.shape[0]
    groups = -(-local // GROUP)
    pad = groups * GROUP - local
    sizes = CHUNKS if sum(CHUNKS) == groups else (groups,)

    sin_polar = jnp.sqrt(1.0 - dir_cos * dir_cos)
    directions = jnp.stack(
        [sin_polar * jnp.cos(dir_phase), sin_polar * jnp.sin(dir_phase), dir_cos], axis=0
    )
    proj = jnp.sum(positions[:, None, :] * directions[:, :, None], axis=0)
    proj = jnp.pad(proj, ((0, pad), (0, 0))).reshape(groups, GROUP, rows)
    factor = jnp.pad(scale * dir_weight, (0, pad))
    node = jnp.asarray((_NODE.astype(np.float64) / (2 * np.pi)).astype(np.float32))[:, None]
    coef = pair_coefs(frequencies)
    mask = (jnp.arange(rows, dtype=jnp.int32) < block_counts[0]).astype(F32)
    qt = (queries.astype(F32) * mask[:, None]).T
    kt = (keys.astype(F32) * mask[:, None]).T
    vh = values.reshape(rows, HEADS, HD).transpose(1, 0, 2)
    ch = cotangent.reshape(rows, HEADS, HD).transpose(1, 0, 2)
    zero = jnp.zeros_like(vh)
    w = jnp.concatenate(
        [jnp.concatenate([vh, zero], 2), jnp.concatenate([zero, ch], 2)], 1
    )
    vt = values.T.reshape(HEADS, HD, rows)
    ct = cotangent.T.reshape(HEADS, HD, rows)
    zero = jnp.zeros_like(vt)
    rhs = jnp.concatenate(
        [jnp.concatenate([ct, zero], 2), jnp.concatenate([zero, vt], 2)], 1
    )

    edges = np.cumsum((0,) + tuple(sizes))
    spans = [(int(a), int(b)) for a, b in zip(edges[:-1], edges[1:])]
    parts = [call_one(proj[a:b], node, coef, qt, kt, w) for a, b in spans]

    if n_atom == SHARDS:
        ring = Ring("atom", n_atom)
        peak = lambda x: jnp.max(jnp.abs(x.astype(F32)).reshape(rows, HEADS, HD), axis=(0, 2))
        bound = jnp.stack([peak(keys) * peak(values), peak(queries) * peak(cotangent)], 1)
        bound = lax.psum(bound, "atom") * (1.5 * rows)
        gain = jnp.exp2(jnp.floor(jnp.log2(60000.0 / jnp.maximum(bound, 1e-30))))
        gain = jnp.repeat(gain, HD, axis=1)
        gain = jnp.repeat(gain, 2, axis=0)
        sums = []
        for (a, b), part in zip(spans, parts):
            scaled = part * gain[:, None, None, :]
            total = ring.scatter_sum(scaled, 1.0)
            mine = lax.dynamic_index_in_dim(gain, ring.me, 0, keepdims=False)
            fac = factor[a * GROUP : b * GROUP]
            total = total * (fac[:, None, None] * (1.0 / mine)[None, None, :])
            sums.append(ring.gather(total.astype(BF16)))
        first = (SHARDS + 4 - ring.me).reshape(1)
    else:
        sums = []
        for (a, b), part in zip(spans, parts):
            fac = factor[a * GROUP : b * GROUP]
            sums.append(lax.psum(part * fac[None, :, None, None], "atom").astype(BF16))
        first = jnp.zeros((1,), jnp.int32)

    grads = [jnp.zeros((width, rows), F32)] * 3
    for (a, b), sg in zip(spans, sums):
        grads = call_two(first, proj[a:b], node, coef, kt, rhs, sg, grads)
    outs = []
    for g in grads:
        other = lax.ppermute(g, "dir", [(0, 1), (1, 0)])
        outs.append(((g + other) * mask[None, :]).astype(BF16).T)
    return tuple(outs)


def solution(mesh):
    in_specs = (
        P(None, ("rep", "atom")),
        P(("rep", "atom"), None),
        P(("rep", "atom"), None),
        P(("rep", "atom"), None),
        P(("rep", "atom"), None),
        P(("rep", "atom")),
        P("dir"),
        P("dir"),
        P("dir"),
        P(),
    )
    out_specs = (P(("rep", "atom"), None), P(("rep", "atom"), None), P(("rep", "atom"), None))
    return jax.shard_map(body, mesh=mesh, in_specs=in_specs, out_specs=out_specs, check_vma=False)
```

```python
import functools
import math

import jax
import jax.numpy as jnp
import numpy as np
from jax import lax
from jax.experimental import pallas as pl
from jax.experimental.pallas import tpu as pltpu
from jax.sharding import PartitionSpec as P

HEADS = 4
HD = 64
HALF = 32
WIDTH = HEADS * HD
NODES = 16
F32 = jnp.float32
BF16 = jnp.bfloat16
F16 = jnp.float16

_NODE = np.cos((np.arange(NODES) + 0.5) * np.pi / (2 * NODES)).astype(np.float32)


def _fit(func, terms):
    z = 0.125 * (1 - np.cos((np.arange(256) + 0.5) * np.pi / 256))
    cheb = np.polynomial.chebyshev.Chebyshev.fit(z, func(z), terms - 1, domain=[0, 0.25])
    return [float(c) for c in cheb.convert(kind=np.polynomial.Polynomial).coef]


_SIN = _fit(lambda z: np.sin(2 * np.pi * np.sqrt(z)) / np.sqrt(z), 7)
_COS = _fit(lambda z: np.cos(2 * np.pi * np.sqrt(z)), 7)


def horner(coef, z):
    acc = coef[-1] * z + coef[-2]
    for c in coef[-3::-1]:
        acc = acc * z + c
    return acc


def pair_coefs(frequencies):
    node = jnp.asarray(_NODE)
    n64 = _NODE.astype(np.float64)
    den = n64[:, None] ** 2 - n64[None, :] ** 2
    np.fill_diagonal(den, 1.0)
    inv = jnp.asarray((1.0 / den).astype(np.float32))
    f = frequencies[:, None]
    num = (f - node) * (f + node)
    fac = jnp.where(jnp.eye(NODES, dtype=bool)[None], 1.0, num[:, None, :] * inv[None])
    cosine = jnp.prod(fac, axis=2)
    sine = cosine * (f / node)
    zero = jnp.zeros_like(cosine)
    full = jnp.concatenate(
        [jnp.concatenate([cosine, zero], 1), jnp.concatenate([zero, sine], 1)], 0
    )
    one = lax.reduce_precision(full, 8, 7)
    two = lax.reduce_precision(full - one, 8, 7)
    three = full - one - two
    return jnp.concatenate([one, two, three, one, two, one], 1).astype(BF16)


def store_features(feat_ref, node_ref, proj_row):
    turns = node_ref[...] * proj_row
    turns = turns - jnp.round(turns)
    z = turns * turns
    full = jnp.concatenate([horner(_COS, z), turns * horner(_SIN, z)], axis=0)
    one = full.astype(BF16)
    rest = full - one.astype(F32)
    two = rest.astype(BF16)
    three = (rest - two.astype(F32)).astype(BF16)
    feat_ref[...] = jnp.concatenate([one, one, one, two, two, three], axis=0)


def pass_one(rows, group, tile, proj_ref, node_ref, coef_ref, qt_ref, kt_ref, w_ref, out_ref, feat_ref, rot_ref):
    def one_group(g, unused):
        for u in range(group):
            store_features(feat_ref, node_ref, proj_ref[g, u : u + 1, :])
            lo = slice(u * HD, u * HD + HALF)
            hi = slice(u * HD + HALF, (u + 1) * HD)
            for t in range(rows // tile):
                at = slice(t * tile, (t + 1) * tile)
                trig = jnp.dot(coef_ref[...], feat_ref[:, at], preferred_element_type=F32)
                for h in range(HEADS):
                    c = trig[h * HALF : (h + 1) * HALF]
                    s = trig[128 + h * HALF : 128 + (h + 1) * HALF]
                    for i, src in enumerate((kt_ref, qt_ref)):
                        to = slice(i * rows + t * tile, i * rows + (t + 1) * tile)
                        a = src[h * HD : h * HD + HALF, at]
                        b = src[h * HD + HALF : (h + 1) * HD, at]
                        rot_ref[h, lo, to] = (a * c - b * s).astype(BF16)
                        rot_ref[h, hi, to] = (a * s + b * c).astype(BF16)
        for h in range(HEADS):
            res = jnp.dot(rot_ref[h], w_ref[h], preferred_element_type=F32)
            for u in range(group):
                out_ref[g * group + u, h * HD : (h + 1) * HD, :] = res[u * HD : (u + 1) * HD]
        return 0

    lax.fori_loop(0, proj_ref.shape[0], one_group, 0)


def pass_two(rows, group, tile, proj_ref, node_ref, coef_ref, kt_ref, rhs_ref, sg_ref, *rest):
    gq_ref, gk_ref, gv_ref, feat_ref, rot_ref, d_ref = rest[-6:]
    if len(rest) == 9:
        gq_ref[...] = rest[0][...]
        gk_ref[...] = rest[1][...]
        gv_ref[...] = rest[2][...]
    else:
        gq_ref[...] = jnp.zeros_like(gq_ref)
        gk_ref[...] = jnp.zeros_like(gk_ref)
        gv_ref[...] = jnp.zeros_like(gv_ref)

    def one_group(g, unused):
        for u in range(group):
            store_features(feat_ref.at[u], node_ref, proj_ref[g, u : u + 1, :])
        gs = []
        for h in range(HEADS):
            sg = jnp.concatenate(
                [sg_ref[g * group + u, h * HD : (h + 1) * HD, :] for u in range(group)], axis=0
            )
            d_ref[h] = jnp.dot(sg, rhs_ref[h], preferred_element_type=F32)
            gs.append(jnp.transpose(sg[:, HD:].astype(F32)).astype(BF16))
        for t in range(rows // tile):
            at = slice(t * tile, (t + 1) * tile)
            at2 = slice(rows + t * tile, rows + (t + 1) * tile)
            for u in range(group):
                trig = jnp.dot(coef_ref[...], feat_ref[u, :, at], preferred_element_type=F32)
                ulo = slice(u * HD, u * HD + HALF)
                uhi = slice(u * HD + HALF, (u + 1) * HD)
                for h in range(HEADS):
                    c = trig[h * HALF : (h + 1) * HALF]
                    s = trig[128 + h * HALF : 128 + (h + 1) * HALF]
                    lo = slice(h * HD, h * HD + HALF)
                    hi = slice(h * HD + HALF, (h + 1) * HD)
                    a = kt_ref[lo, at]
                    b = kt_ref[hi, at]
                    rot_ref[h, ulo, at] = (a * c - b * s).astype(BF16)
                    rot_ref[h, uhi, at] = (a * s + b * c).astype(BF16)
                    a = d_ref[h, ulo, at]
                    b = d_ref[h, uhi, at]
                    gq_ref[lo, at] += a * c + b * s
                    gq_ref[hi, at] += b * c - a * s
                    a = d_ref[h, ulo, at2]
                    b = d_ref[h, uhi, at2]
                    gk_ref[lo, at] += a * c + b * s
                    gk_ref[hi, at] += b * c - a * s
        for h in range(HEADS):
            gv_ref[h * HD : (h + 1) * HD, :] += jnp.dot(
                gs[h], rot_ref[h], preferred_element_type=F32
            )
        return 0

    lax.fori_loop(0, proj_ref.shape[0], one_group, 0)


VMEM = pl.BlockSpec(memory_space=pltpu.VMEM)


def call_one(proj, node, coef, qt, kt, w, tile=256):
    groups, group, rows = proj.shape
    return pl.pallas_call(
        functools.partial(pass_one, rows, group, tile),
        name="pass_one",
        in_specs=[VMEM] * 6,
        out_specs=VMEM,
        out_shape=jax.ShapeDtypeStruct((groups * group, WIDTH, 128), F32),
        scratch_shapes=[
            pltpu.VMEM((192, rows), BF16),
            pltpu.VMEM((HEADS, group * HD, 2 * rows), BF16),
        ],
        compiler_params=pltpu.CompilerParams(vmem_limit_bytes=24 << 20),
    )(proj, node, coef, qt, kt, w)


def call_two(proj, node, coef, kt, rhs, sg, grads, tile=128):
    groups, group, rows = proj.shape
    out = jax.ShapeDtypeStruct((WIDTH, rows), F32)
    return pl.pallas_call(
        functools.partial(pass_two, rows, group, tile),
        name="pass_two",
        in_specs=[VMEM] * (6 + len(grads)),
        out_specs=[VMEM] * 3,
        out_shape=[out] * 3,
        scratch_shapes=[
            pltpu.VMEM((group, 192, rows), BF16),
            pltpu.VMEM((HEADS, group * HD, rows), BF16),
            pltpu.VMEM((HEADS, group * HD, 2 * rows), F32),
        ],
        input_output_aliases={6 + i: i for i in range(len(grads))},
        compiler_params=pltpu.CompilerParams(vmem_limit_bytes=40 << 20),
    )(proj, node, coef, kt, rhs, sg, *grads)


RING = (0, 2, 4, 6, 7, 5, 3, 1)
UP = tuple((RING[i], RING[(i + 1) % 8]) for i in range(8))
DOWN = tuple((b, a) for a, b in UP)
TOP = 60000.0


def send(up, down):
    return lax.ppermute(up, "atom", UP), lax.ppermute(down, "atom", DOWN)


def pack(part, bound):
    code = jnp.floor(jnp.log2(TOP / bound))
    n = part.shape[0]
    data = part.reshape(n, HEADS, HD, 128) * jnp.exp2(code)[None, :, None, :]
    rows = jnp.concatenate([data.reshape(n * WIDTH, 128), jnp.tile(code, (4, 1))], 0)
    return rows.astype(F16)


def unpack(got):
    code = got[-HEADS:].astype(F32)
    data = got[:-16].astype(F32).reshape(-1, HEADS, HD, 128)
    data = data * jnp.exp2(-code)[None, :, None, :]
    return data.reshape(-1, WIDTH, 128), TOP * jnp.exp2(-code)


def body(
    positions,
    queries,
    keys,
    values,
    cotangent,
    block_counts,
    dir_cos,
    dir_phase,
    dir_weight,
    frequencies,
):
    rows = queries.shape[0]
    n_atom = lax.axis_size("atom")
    scale = 1.0 / (8.0 * math.sqrt(rows * n_atom))
    local = dir_cos.shape[0]
    group = -(-local // 8)
    ringed = n_atom == 8
    table = jnp.stack([dir_cos, dir_phase, dir_weight], 0)
    table = jnp.pad(table, ((0, 0), (0, 8 * group - local))).reshape(3, 8, group)
    if ringed:
        where = np.argsort(np.array(RING)).astype(np.int32)
        place = jnp.asarray(where)[lax.axis_index("atom")]
        table = lax.dynamic_slice_in_dim(jnp.concatenate([table, table], 1), place, 8, 1)
    cosine, phase, weight = table
    sin_polar = jnp.sqrt(1.0 - cosine * cosine)
    directions = jnp.stack([sin_polar * jnp.cos(phase), sin_polar * jnp.sin(phase), cosine], 0)
    proj = jnp.sum(positions[:, None, None, :] * directions[:, :, :, None], axis=0)
    factor = scale * weight
    node = jnp.asarray((_NODE.astype(np.float64) / (2 * np.pi)).astype(np.float32))[:, None]
    coef = pair_coefs(frequencies)
    mask = (jnp.arange(rows, dtype=jnp.int32) < block_counts[0]).astype(F32)
    qt = (queries.astype(F32) * mask[:, None]).T
    kt = (keys.astype(F32) * mask[:, None]).T
    vh = values.reshape(rows, HEADS, HD).transpose(1, 0, 2)
    ch = cotangent.reshape(rows, HEADS, HD).transpose(1, 0, 2)
    zero = jnp.zeros_like(vh)
    w = jnp.concatenate(
        [jnp.concatenate([vh, zero], 2), jnp.concatenate([zero, ch], 2)], 1
    )
    vt = values.T.reshape(HEADS, HD, rows)
    ct = cotangent.T.reshape(HEADS, HD, rows)
    zero = jnp.zeros_like(vt)
    rhs = jnp.concatenate(
        [jnp.concatenate([ct, zero], 2), jnp.concatenate([zero, vt], 2)], 1
    )

    def one(*shards, after=()):
        picked = jnp.stack([proj[j % 8] for j in shards], 0)
        picked, after = lax.optimization_barrier((picked, after))
        return call_one(picked, node, coef, qt, kt, w)

    def two(sg, shards, grads):
        picked = jnp.stack([proj[j % 8] for j in shards], 0)
        return call_two(picked, node, coef, kt, rhs, sg, grads)

    if ringed:
        peak = lambda x: jnp.max(jnp.abs(x.astype(F32)).reshape(rows, HEADS, HD), axis=(0, 2))
        bound = jnp.stack([peak(keys) * peak(values), peak(queries) * peak(cotangent)], 1)
        bound = jnp.repeat(bound * (1.5 * rows) + 1e-9, HD, axis=1)
        half = group // 2
        part = one(4)
        ready = pack(part[:half], bound), pack(part[half:], bound)
        for ahead in (3, 2, 1):
            last = send(*ready)
            part = one(ahead, -ahead, after=ready)
            up, down = part[:group], part[group:]
            (got_up, up_bound), (got_down, down_bound) = unpack(last[0]), unpack(last[1])
            if ahead == 3:
                got_up = jnp.pad(got_up, ((0, group - half), (0, 0), (0, 0)))
                got_down = jnp.pad(got_down, ((half, 0), (0, 0), (0, 0)))
            ready = pack(up + got_up, bound + up_bound), pack(down + got_down, bound + down_bound)
        last = send(*ready)
        total = one(0, after=ready) + unpack(last[0])[0] + unpack(last[1])[0]
        mine = (total * factor[0][:, None, None]).astype(BF16)
        up, down = send(mine, mine)
        grads = two(mine, (0,), ())
        for ahead in (1, 2, 3):
            up, down, grads = lax.optimization_barrier((up, down, grads))
            both = jnp.concatenate([up, down], 0)
            if ahead < 3:
                up, down = send(up, down)
            else:
                up, down = send(up[:half], down[half:])
            grads = two(both, (-ahead, ahead), grads)
        grads = two(jnp.concatenate([up, down], 0), (4,), grads)
    else:
        part = one(*range(8)) * factor.reshape(-1)[:, None, None]
        grads = two(lax.psum(part, "atom").astype(BF16), range(8), ())
    outs = []
    for g in grads:
        other = lax.ppermute(g, "dir", [(0, 1), (1, 0)])
        outs.append(((g + other) * mask[None, :]).astype(BF16).T)
    return tuple(outs)


def solution(mesh):
    in_specs = (
        P(None, ("rep", "atom")),
        P(("rep", "atom"), None),
        P(("rep", "atom"), None),
        P(("rep", "atom"), None),
        P(("rep", "atom"), None),
        P(("rep", "atom")),
        P("dir"),
        P("dir"),
        P("dir"),
        P(),
    )
    out_specs = (P(("rep", "atom"), None), P(("rep", "atom"), None), P(("rep", "atom"), None))
    return jax.shard_map(body, mesh=mesh, in_specs=in_specs, out_specs=out_specs, check_vma=False)
```

```python
import functools
import math

import jax
import jax.numpy as jnp
import numpy as np
from jax import lax
from jax.experimental import pallas as pl
from jax.experimental.pallas import tpu as pltpu
from jax.sharding import PartitionSpec as P

HEADS = 4
HD = 64
HALF = 32
WIDTH = HEADS * HD
NODES = 16
F32 = jnp.float32
BF16 = jnp.bfloat16
F16 = jnp.float16

_NODE = np.cos((np.arange(NODES) + 0.5) * np.pi / (2 * NODES)).astype(np.float32)


def _fit(func, terms):
    z = 0.125 * (1 - np.cos((np.arange(256) + 0.5) * np.pi / 256))
    cheb = np.polynomial.chebyshev.Chebyshev.fit(z, func(z), terms - 1, domain=[0, 0.25])
    return [float(c) for c in cheb.convert(kind=np.polynomial.Polynomial).coef]


_SIN = _fit(lambda z: np.sin(2 * np.pi * np.sqrt(z)) / np.sqrt(z), 7)
_COS = _fit(lambda z: np.cos(2 * np.pi * np.sqrt(z)), 7)


def horner(coef, z):
    acc = coef[-1] * z + coef[-2]
    for c in coef[-3::-1]:
        acc = acc * z + c
    return acc


def pair_coefs(frequencies):
    node = jnp.asarray(_NODE)
    n64 = _NODE.astype(np.float64)
    den = n64[:, None] ** 2 - n64[None, :] ** 2
    np.fill_diagonal(den, 1.0)
    inv = jnp.asarray((1.0 / den).astype(np.float32))
    f = frequencies[:, None]
    num = (f - node) * (f + node)
    fac = jnp.where(jnp.eye(NODES, dtype=bool)[None], 1.0, num[:, None, :] * inv[None])
    cosine = jnp.prod(fac, axis=2)
    sine = cosine * (f / node)
    zero = jnp.zeros_like(cosine)
    full = jnp.concatenate(
        [jnp.concatenate([cosine, zero], 1), jnp.concatenate([zero, sine], 1)], 0
    )
    one = lax.reduce_precision(full, 8, 7)
    two = lax.reduce_precision(full - one, 8, 7)
    three = full - one - two
    return jnp.concatenate([one, two, three, one, two, one], 1).astype(BF16)


def store_features(feat_ref, node_ref, proj_row):
    turns = node_ref[...] * proj_row
    turns = turns - jnp.round(turns)
    z = turns * turns
    full = jnp.concatenate([horner(_COS, z), turns * horner(_SIN, z)], axis=0)
    one = full.astype(BF16)
    rest = full - one.astype(F32)
    two = rest.astype(BF16)
    three = (rest - two.astype(F32)).astype(BF16)
    feat_ref[...] = jnp.concatenate([one, one, one, two, two, three], axis=0)


def pass_one(rows, group, tile, proj_ref, node_ref, coef_ref, qt_ref, kt_ref, w_ref, out_ref, feat_ref, rot_ref):
    def one_group(g, unused):
        for u in range(group):
            store_features(feat_ref, node_ref, proj_ref[g, u : u + 1, :])
            lo = slice(u * HD, u * HD + HALF)
            hi = slice(u * HD + HALF, (u + 1) * HD)
            for t in range(rows // tile):
                at = slice(t * tile, (t + 1) * tile)
                trig = jnp.dot(coef_ref[...], feat_ref[:, at], preferred_element_type=F32)
                for h in range(HEADS):
                    c = trig[h * HALF : (h + 1) * HALF]
                    s = trig[128 + h * HALF : 128 + (h + 1) * HALF]
                    for i, src in enumerate((kt_ref, qt_ref)):
                        to = slice(i * rows + t * tile, i * rows + (t + 1) * tile)
                        a = src[h * HD : h * HD + HALF, at]
                        b = src[h * HD + HALF : (h + 1) * HD, at]
                        rot_ref[h, lo, to] = (a * c - b * s).astype(BF16)
                        rot_ref[h, hi, to] = (a * s + b * c).astype(BF16)
        for h in range(HEADS):
            res = jnp.dot(rot_ref[h], w_ref[h], preferred_element_type=F32)
            for u in range(group):
                out_ref[g * group + u, h * HD : (h + 1) * HD, :] = res[u * HD : (u + 1) * HD]
        return 0

    lax.fori_loop(0, proj_ref.shape[0], one_group, 0)


def pass_two(rows, group, tile, proj_ref, node_ref, coef_ref, kt_ref, rhs_ref, sg_ref, *rest):
    gq_ref, gk_ref, gv_ref, feat_ref, rot_ref, gst_ref, *pairs = rest[-10:]
    trig_refs, d_refs = pairs[:2], pairs[2:]
    if len(rest) == 13:
        gq_ref[...] = rest[0][...]
        gk_ref[...] = rest[1][...]
        gv_ref[...] = rest[2][...]
    else:
        gq_ref[...] = jnp.zeros_like(gq_ref)
        gk_ref[...] = jnp.zeros_like(gk_ref)
        gv_ref[...] = jnp.zeros_like(gv_ref)
    groups = proj_ref.shape[0]
    per = rows // tile
    total = groups * per

    def stacked(g, h):
        return jnp.concatenate(
            [sg_ref[g * group + u, h * HD : (h + 1) * HD, :] for u in range(group)], axis=0
        )

    for g in range(groups):
        for h in range(HEADS):
            gst_ref[g, h] = jnp.transpose(stacked(g, h)[:, HD:].astype(F32)).astype(BF16)

    def where(i):
        base = (i % per) * tile
        if not isinstance(i, int):
            base = pl.multiple_of(base, tile)
        return i // per, base

    def first(i, slot):
        g, base = where(i)

        def trig(u):
            store_features(feat_ref.at[u], node_ref, proj_ref[g, pl.ds(u, 1), pl.ds(base, tile)])
            trig_refs[slot][u] = jnp.dot(coef_ref[...], feat_ref[u], preferred_element_type=F32)

        def rotated(h, side):
            at = pl.ds(base + side * rows, tile)
            d_refs[slot][h, side] = jnp.dot(
                stacked(g, h), rhs_ref[h, :, at], preferred_element_type=F32
            )

        units = []
        for k in range(2 * HEADS):
            units.append([functools.partial(rotated, k // 2, k % 2)])
            if k < group:
                units[-1].append(functools.partial(trig, k))
        for u in range(2 * HEADS, group):
            units[-1].append(functools.partial(trig, u))
        return units

    def second(i, slot):
        g, base = where(i)
        at = pl.ds(base, tile)
        trig_ref, d_ref = trig_refs[slot], d_refs[slot]

        def head(h):
            lo = slice(h * HD, h * HD + HALF)
            hi = slice(h * HD + HALF, (h + 1) * HD)
            ka, kb = kt_ref[lo, at], kt_ref[hi, at]
            qa, qb, va, vb = gq_ref[lo, at], gq_ref[hi, at], gk_ref[lo, at], gk_ref[hi, at]
            for u in range(group):
                c = trig_ref[u, h * HALF : (h + 1) * HALF, :]
                s = trig_ref[u, 128 + h * HALF : 128 + (h + 1) * HALF, :]
                ulo = slice(u * HD, u * HD + HALF)
                uhi = slice(u * HD + HALF, (u + 1) * HD)
                rot_ref[h, ulo, :] = (ka * c - kb * s).astype(BF16)
                rot_ref[h, uhi, :] = (ka * s + kb * c).astype(BF16)
                a, b = d_ref[h, 0, ulo, :], d_ref[h, 0, uhi, :]
                qa, qb = qa + (a * c + b * s), qb + (b * c - a * s)
                a, b = d_ref[h, 1, ulo, :], d_ref[h, 1, uhi, :]
                va, vb = va + (a * c + b * s), vb + (b * c - a * s)
            gq_ref[lo, at], gq_ref[hi, at], gk_ref[lo, at], gk_ref[hi, at] = qa, qb, va, vb
            gv_ref[h * HD : (h + 1) * HD, at] += jnp.dot(
                gst_ref[g, h], rot_ref[h], preferred_element_type=F32
            )

        return [[functools.partial(head, k // 2)] if k % 2 else [] for k in range(2 * HEADS)]

    def run(*stages):
        for units in zip(*stages):
            for unit in units:
                for step in unit:
                    step()

    run(first(0, 0))

    def two_tiles(j, unused):
        run(first(2 * j + 1, 1), second(2 * j, 0))
        run(first(jnp.minimum(2 * j + 2, total - 1), 0), second(2 * j + 1, 1))
        return 0

    lax.fori_loop(0, total // 2, two_tiles, 0)


VMEM = pl.BlockSpec(memory_space=pltpu.VMEM)


def call_one(proj, node, coef, qt, kt, w, tile=256):
    groups, group, rows = proj.shape
    return pl.pallas_call(
        functools.partial(pass_one, rows, group, tile),
        name="pass_one",
        in_specs=[VMEM] * 6,
        out_specs=VMEM,
        out_shape=jax.ShapeDtypeStruct((groups * group, WIDTH, 128), F32),
        scratch_shapes=[
            pltpu.VMEM((192, rows), BF16),
            pltpu.VMEM((HEADS, group * HD, 2 * rows), BF16),
        ],
        compiler_params=pltpu.CompilerParams(vmem_limit_bytes=24 << 20),
    )(proj, node, coef, qt, kt, w)


def call_two(proj, node, coef, kt, rhs, sg, grads, tile=256):
    groups, group, rows = proj.shape
    out = jax.ShapeDtypeStruct((WIDTH, rows), F32)
    return pl.pallas_call(
        functools.partial(pass_two, rows, group, tile),
        name="pass_two",
        in_specs=[VMEM] * (6 + len(grads)),
        out_specs=[VMEM] * 3,
        out_shape=[out] * 3,
        scratch_shapes=[
            pltpu.VMEM((group, 192, tile), BF16),
            pltpu.VMEM((HEADS, group * HD, tile), BF16),
            pltpu.VMEM((groups, HEADS, HD, group * HD), BF16),
            pltpu.VMEM((group, WIDTH, tile), F32),
            pltpu.VMEM((group, WIDTH, tile), F32),
            pltpu.VMEM((HEADS, 2, group * HD, tile), F32),
            pltpu.VMEM((HEADS, 2, group * HD, tile), F32),
        ],
        input_output_aliases={6 + i: i for i in range(len(grads))},
        compiler_params=pltpu.CompilerParams(vmem_limit_bytes=28 << 20),
    )(proj, node, coef, kt, rhs, sg, *grads)


RING = (0, 2, 4, 6, 7, 5, 3, 1)
UP = tuple((RING[i], RING[(i + 1) % 8]) for i in range(8))
DOWN = tuple((b, a) for a, b in UP)
TOP = 60000.0


def send(up, down):
    return lax.ppermute(up, "atom", UP), lax.ppermute(down, "atom", DOWN)


def pack(part, bound):
    code = jnp.floor(jnp.log2(TOP / bound))
    n = part.shape[0]
    data = part.reshape(n, HEADS, HD, 128) * jnp.exp2(code)[None, :, None, :]
    rows = jnp.concatenate([data.reshape(n * WIDTH, 128), jnp.tile(code, (4, 1))], 0)
    return rows.astype(F16)


def unpack(got):
    code = got[-HEADS:].astype(F32)
    data = got[:-16].astype(F32).reshape(-1, HEADS, HD, 128)
    data = data * jnp.exp2(-code)[None, :, None, :]
    return data.reshape(-1, WIDTH, 128), TOP * jnp.exp2(-code)


def body(
    positions,
    queries,
    keys,
    values,
    cotangent,
    block_counts,
    dir_cos,
    dir_phase,
    dir_weight,
    frequencies,
):
    rows = queries.shape[0]
    n_atom = lax.axis_size("atom")
    scale = 1.0 / (8.0 * math.sqrt(rows * n_atom))
    local = dir_cos.shape[0]
    group = -(-local // 8)
    ringed = n_atom == 8
    table = jnp.stack([dir_cos, dir_phase, dir_weight], 0)
    table = jnp.pad(table, ((0, 0), (0, 8 * group - local))).reshape(3, 8, group)
    if ringed:
        where = np.argsort(np.array(RING)).astype(np.int32)
        place = jnp.asarray(where)[lax.axis_index("atom")]
        table = lax.dynamic_slice_in_dim(jnp.concatenate([table, table], 1), place, 8, 1)
    cosine, phase, weight = table
    sin_polar = jnp.sqrt(1.0 - cosine * cosine)
    directions = jnp.stack([sin_polar * jnp.cos(phase), sin_polar * jnp.sin(phase), cosine], 0)
    proj = jnp.sum(positions[:, None, None, :] * directions[:, :, :, None], axis=0)
    factor = scale * weight
    node = jnp.asarray((_NODE.astype(np.float64) / (2 * np.pi)).astype(np.float32))[:, None]
    coef = pair_coefs(frequencies)
    mask = (jnp.arange(rows, dtype=jnp.int32) < block_counts[0]).astype(F32)
    qt = (queries.astype(F32) * mask[:, None]).T
    kt = (keys.astype(F32) * mask[:, None]).T
    vh = values.reshape(rows, HEADS, HD).transpose(1, 0, 2)
    ch = cotangent.reshape(rows, HEADS, HD).transpose(1, 0, 2)
    zero = jnp.zeros_like(vh)
    w = jnp.concatenate(
        [jnp.concatenate([vh, zero], 2), jnp.concatenate([zero, ch], 2)], 1
    )
    vt = values.T.reshape(HEADS, HD, rows)
    ct = cotangent.T.reshape(HEADS, HD, rows)
    zero = jnp.zeros_like(vt)
    rhs = jnp.concatenate(
        [jnp.concatenate([ct, zero], 2), jnp.concatenate([zero, vt], 2)], 1
    )

    def one(*shards, after=()):
        picked = jnp.stack([proj[j % 8] for j in shards], 0)
        picked, after = lax.optimization_barrier((picked, after))
        return call_one(picked, node, coef, qt, kt, w)

    def two(sg, shards, grads):
        picked = jnp.stack([proj[j % 8] for j in shards], 0)
        return call_two(picked, node, coef, kt, rhs, sg, grads)

    if ringed:
        peak = lambda x: jnp.max(jnp.abs(x.astype(F32)).reshape(rows, HEADS, HD), axis=(0, 2))
        bound = jnp.stack([peak(keys) * peak(values), peak(queries) * peak(cotangent)], 1)
        bound = jnp.repeat(bound * (1.5 * rows) + 1e-9, HD, axis=1)
        half = group // 2
        part = one(4)
        ready = pack(part[:half], bound), pack(part[half:], bound)
        for ahead in (3, 2, 1):
            last = send(*ready)
            part = one(ahead, -ahead, after=ready)
            up, down = part[:group], part[group:]
            (got_up, up_bound), (got_down, down_bound) = unpack(last[0]), unpack(last[1])
            if ahead == 3:
                got_up = jnp.pad(got_up, ((0, group - half), (0, 0), (0, 0)))
                got_down = jnp.pad(got_down, ((half, 0), (0, 0), (0, 0)))
            ready = pack(up + got_up, bound + up_bound), pack(down + got_down, bound + down_bound)
        last = send(*ready)
        total = one(0, after=ready) + unpack(last[0])[0] + unpack(last[1])[0]
        mine = (total * factor[0][:, None, None]).astype(BF16)
        up, down = send(mine, mine)
        grads = two(mine, (0,), ())
        for ahead in (1, 2, 3):
            up, down, grads = lax.optimization_barrier((up, down, grads))
            both = jnp.concatenate([up, down], 0)
            if ahead < 3:
                up, down = send(up, down)
            else:
                up, down = send(up[:half], down[half:])
            grads = two(both, (-ahead, ahead), grads)
        grads = two(jnp.concatenate([up, down], 0), (4,), grads)
    else:
        part = one(*range(8)) * factor.reshape(-1)[:, None, None]
        grads = two(lax.psum(part, "atom").astype(BF16), range(8), ())
    outs = []
    for g in grads:
        other = lax.ppermute(g, "dir", [(0, 1), (1, 0)])
        outs.append(((g + other) * mask[None, :]).astype(BF16).T)
    return tuple(outs)


def solution(mesh):
    in_specs = (
        P(None, ("rep", "atom")),
        P(("rep", "atom"), None),
        P(("rep", "atom"), None),
        P(("rep", "atom"), None),
        P(("rep", "atom"), None),
        P(("rep", "atom")),
        P("dir"),
        P("dir"),
        P("dir"),
        P(),
    )
    out_specs = (P(("rep", "atom"), None), P(("rep", "atom"), None), P(("rep", "atom"), None))
    return jax.shard_map(body, mesh=mesh, in_specs=in_specs, out_specs=out_specs, check_vma=False)
```

```python
import functools
import math

import jax
import jax.numpy as jnp
import numpy as np
from jax import lax
from jax.experimental import pallas as pl
from jax.experimental.pallas import tpu as pltpu
from jax.sharding import PartitionSpec as P

HEADS = 4
HD = 64
HALF = 32
WIDTH = HEADS * HD
NODES = 16
F32 = jnp.float32
BF16 = jnp.bfloat16
F16 = jnp.float16

_NODE = np.cos((np.arange(NODES) + 0.5) * np.pi / (2 * NODES)).astype(np.float32)


def _fit(func, terms):
    z = 0.125 * (1 - np.cos((np.arange(256) + 0.5) * np.pi / 256))
    cheb = np.polynomial.chebyshev.Chebyshev.fit(z, func(z), terms - 1, domain=[0, 0.25])
    return [float(c) for c in cheb.convert(kind=np.polynomial.Polynomial).coef]


_SIN = _fit(lambda z: np.sin(2 * np.pi * np.sqrt(z)) / np.sqrt(z), 7)
_COS = _fit(lambda z: np.cos(2 * np.pi * np.sqrt(z)), 7)


def horner(coef, z):
    acc = coef[-1] * z + coef[-2]
    for c in coef[-3::-1]:
        acc = acc * z + c
    return acc


def store_coefs(coef_ref, full_ref, f):
    n64 = _NODE.astype(np.float64)
    nums = [(f - float(x)) * (f + float(x)) for x in _NODE]
    before, after = [None], [None]
    for i in range(NODES - 1):
        before.append(nums[i] if i == 0 else before[-1] * nums[i])
        k = NODES - 1 - i
        after.append(nums[k] if i == 0 else after[-1] * nums[k])
    after = after[::-1]
    full_ref[...] = jnp.zeros_like(full_ref)
    for j in range(NODES):
        den = np.delete(n64[j] ** 2 - n64**2, j)
        lead = before[j] if after[j] is None else after[j]
        if before[j] is not None and after[j] is not None:
            lead = before[j] * after[j]
        cosine = lead * float(1.0 / np.prod(den))
        full_ref[j : j + 1, :128] = cosine
        full_ref[NODES + j : NODES + j + 1, 128:] = cosine * (f * float(1.0 / n64[j]))
    full = full_ref[...]
    one = full.astype(BF16).astype(F32)
    two = (full - one).astype(BF16).astype(F32)
    three = full - one - two
    stacked = jnp.concatenate([one, two, three, one, two, one], 0)
    coef_ref[...] = jnp.transpose(stacked).astype(BF16)


def store_features(feat_ref, node_ref, proj_row):
    turns = node_ref[...] * proj_row
    turns = turns - jnp.round(turns)
    z = turns * turns
    full = jnp.concatenate([horner(_COS, z), turns * horner(_SIN, z)], axis=0)
    one = full.astype(BF16)
    rest = full - one.astype(F32)
    two = rest.astype(BF16)
    three = (rest - two.astype(F32)).astype(BF16)
    feat_ref[...] = jnp.concatenate([one, one, one, two, two, three], axis=0)


def prepare(rows, scale, count_ref, q_ref, k_ref, v_ref, d_ref, pos_ref, cos_ref, phase_ref, weight_ref, freq_ref, qt_ref, kt_ref, w_ref, rhs_ref, bound_ref, proj_ref, fac_ref, coef_ref, table_ref, full_ref):
    store_coefs(coef_ref, full_ref, freq_ref[...])
    local = cos_ref.shape[1]
    cosine, phase = cos_ref[...], phase_ref[...]
    sin_polar = jnp.sqrt(1.0 - cosine * cosine)
    table_ref[...] = jnp.zeros_like(table_ref)
    table_ref[0:1, :local] = sin_polar * jnp.cos(phase)
    table_ref[1:2, :local] = sin_polar * jnp.sin(phase)
    table_ref[2:3, :local] = cosine
    table_ref[3:4, :local] = scale * weight_ref[...]
    table = jnp.transpose(table_ref[...])[: proj_ref.shape[0]]
    proj_ref[...] = (
        table[:, 0:1] * pos_ref[0:1, :] + table[:, 1:2] * pos_ref[1:2, :] + table[:, 2:3] * pos_ref[2:3, :]
    )
    fac_ref[...] = jnp.broadcast_to(table[:, 3:4], fac_ref.shape)
    mask = (lax.broadcasted_iota(jnp.int32, (1, rows), 1) < count_ref[0]).astype(F32)
    lane = lax.broadcasted_iota(jnp.int32, (1, 128), 1)
    qt = jnp.transpose(q_ref[...].astype(F32)) * mask
    kt = jnp.transpose(k_ref[...].astype(F32)) * mask
    qt_ref[...] = qt
    kt_ref[...] = kt
    vt = jnp.transpose(v_ref[...].astype(F32))
    dt = jnp.transpose(d_ref[...].astype(F32))
    rhs_ref[...] = jnp.zeros_like(rhs_ref)
    zero = jnp.zeros((rows, HD), BF16)
    for h in range(HEADS):
        at = slice(h * HD, (h + 1) * HD)
        rhs_ref[h, :HD, :rows] = dt[at].astype(BF16)
        rhs_ref[h, HD:, rows:] = vt[at].astype(BF16)
        w_ref[h, :rows, :] = jnp.concatenate([v_ref[:, at], zero], 1)
        w_ref[h, rows:, :] = jnp.concatenate([zero, d_ref[:, at]], 1)

        def peak(x):
            most = jnp.max(jnp.abs(x[at]), axis=0, keepdims=True)
            return jnp.max(most, axis=1, keepdims=True)

        most = jnp.where(lane < HD, peak(kt) * peak(vt), peak(qt) * peak(dt))
        bound_ref[h : h + 1, :] = most * (1.5 * rows) + 1e-9


def finish(rows, count_ref, *refs):
    mask = (lax.broadcasted_iota(jnp.int32, (1, rows), 1) < count_ref[0]).astype(F32)
    for mine, other, out in zip(refs[:3], refs[3:6], refs[6:]):
        out[...] = jnp.transpose((mine[...] + other[...]) * mask).astype(BF16)


def shard_at(place_ref, shards, g):
    ahead = shards[-1] % 8
    for i in range(len(shards) - 2, -1, -1):
        ahead = jnp.where(g == i, shards[i] % 8, ahead)
    return lax.rem(place_ref[0] + ahead, 8)


def pass_one(rows, shards, group, tile, place_ref, proj_ref, node_ref, coef_ref, qt_ref, kt_ref, w_ref, out_ref, feat_ref, *rot_refs):
    per = rows // tile

    def one_group(g, unused):
        row = shard_at(place_ref, shards, g) * group

        def rotated(t):
            rot_ref = rot_refs[t % 2]
            at = slice(t * tile, (t + 1) * tile)
            for u in range(group):
                store_features(feat_ref.at[u], node_ref, proj_ref[pl.ds(row + u, 1), at])
            for u in range(group):
                trig = jnp.dot(coef_ref[...], feat_ref[u], preferred_element_type=F32)
                lo = slice(u * HD, u * HD + HALF)
                hi = slice(u * HD + HALF, (u + 1) * HD)
                for h in range(HEADS):
                    c = trig[h * HALF : (h + 1) * HALF]
                    s = trig[128 + h * HALF : 128 + (h + 1) * HALF]
                    for i, src in enumerate((kt_ref, qt_ref)):
                        to = slice(i * tile, (i + 1) * tile)
                        a = src[h * HD : h * HD + HALF, at]
                        b = src[h * HD + HALF : (h + 1) * HD, at]
                        rot_ref[h, lo, to] = (a * c - b * s).astype(BF16)
                        rot_ref[h, hi, to] = (a * s + b * c).astype(BF16)

        def summed(t):
            for h in range(HEADS):
                w = jnp.concatenate(
                    [w_ref[h, i * rows + t * tile : i * rows + (t + 1) * tile, :] for i in range(2)], 0
                )
                res = jnp.dot(rot_refs[t % 2][h], w, preferred_element_type=F32)
                for u in range(group):
                    part = res[u * HD : (u + 1) * HD]
                    if t == 0:
                        out_ref[g * group + u, h * HD : (h + 1) * HD, :] = part
                    else:
                        out_ref[g * group + u, h * HD : (h + 1) * HD, :] += part

        rotated(0)
        for t in range(1, per):
            rotated(t)
            summed(t - 1)
        summed(per - 1)
        return 0

    lax.fori_loop(0, len(shards), one_group, 0)


def pass_two(rows, shards, group, tile, place_ref, proj_ref, node_ref, coef_ref, kt_ref, rhs_ref, sg_ref, *rest):
    gq_ref, gk_ref, gv_ref, feat_ref, rot_ref, gst_ref, *pairs = rest[-10:]
    trig_refs, d_refs = pairs[:2], pairs[2:]
    if len(rest) == 13:
        gq_ref[...] = rest[0][...]
        gk_ref[...] = rest[1][...]
        gv_ref[...] = rest[2][...]
    else:
        gq_ref[...] = jnp.zeros_like(gq_ref)
        gk_ref[...] = jnp.zeros_like(gk_ref)
        gv_ref[...] = jnp.zeros_like(gv_ref)
    groups = len(shards)
    per = rows // tile
    total = groups * per

    def stacked(g, h):
        return jnp.concatenate(
            [sg_ref[g * group + u, h * HD : (h + 1) * HD, :] for u in range(group)], axis=0
        )

    for g in range(groups):
        for h in range(HEADS):
            gst_ref[g, h] = jnp.transpose(stacked(g, h)[:, HD:].astype(F32)).astype(BF16)

    def where(i):
        base = (i % per) * tile
        if not isinstance(i, int):
            base = pl.multiple_of(base, tile)
        return i // per, base

    def first(i, slot):
        g, base = where(i)
        row = shard_at(place_ref, shards, g) * group

        def trig(u):
            at = pl.ds(base, tile)
            store_features(feat_ref.at[u], node_ref, proj_ref[pl.ds(row + u, 1), at])
            trig_refs[slot][u] = jnp.dot(coef_ref[...], feat_ref[u], preferred_element_type=F32)

        def rotated(h, side):
            at = pl.ds(base + side * rows, tile)
            d_refs[slot][h, side] = jnp.dot(
                stacked(g, h), rhs_ref[h, :, at], preferred_element_type=F32
            )

        units = []
        for k in range(2 * HEADS):
            units.append([functools.partial(rotated, k // 2, k % 2)])
            if k < group:
                units[-1].append(functools.partial(trig, k))
        for u in range(2 * HEADS, group):
            units[-1].append(functools.partial(trig, u))
        return units

    def second(i, slot):
        g, base = where(i)
        at = pl.ds(base, tile)
        trig_ref, d_ref = trig_refs[slot], d_refs[slot]

        def head(h):
            lo = slice(h * HD, h * HD + HALF)
            hi = slice(h * HD + HALF, (h + 1) * HD)
            ka, kb = kt_ref[lo, at], kt_ref[hi, at]
            qa, qb, va, vb = gq_ref[lo, at], gq_ref[hi, at], gk_ref[lo, at], gk_ref[hi, at]
            for u in range(group):
                c = trig_ref[u, h * HALF : (h + 1) * HALF, :]
                s = trig_ref[u, 128 + h * HALF : 128 + (h + 1) * HALF, :]
                ulo = slice(u * HD, u * HD + HALF)
                uhi = slice(u * HD + HALF, (u + 1) * HD)
                rot_ref[h, ulo, :] = (ka * c - kb * s).astype(BF16)
                rot_ref[h, uhi, :] = (ka * s + kb * c).astype(BF16)
                a, b = d_ref[h, 0, ulo, :], d_ref[h, 0, uhi, :]
                qa, qb = qa + (a * c + b * s), qb + (b * c - a * s)
                a, b = d_ref[h, 1, ulo, :], d_ref[h, 1, uhi, :]
                va, vb = va + (a * c + b * s), vb + (b * c - a * s)
            gq_ref[lo, at], gq_ref[hi, at], gk_ref[lo, at], gk_ref[hi, at] = qa, qb, va, vb
            gv_ref[h * HD : (h + 1) * HD, at] += jnp.dot(
                gst_ref[g, h], rot_ref[h], preferred_element_type=F32
            )

        return [[functools.partial(head, k // 2)] if k % 2 else [] for k in range(2 * HEADS)]

    def run(*stages):
        for units in zip(*stages):
            for unit in units:
                for step in unit:
                    step()

    run(first(0, 0))

    def two_tiles(j, unused):
        run(first(2 * j + 1, 1), second(2 * j, 0))
        run(first(jnp.minimum(2 * j + 2, total - 1), 0), second(2 * j + 1, 1))
        return 0

    lax.fori_loop(0, total // 2, two_tiles, 0)


VMEM = pl.BlockSpec(memory_space=pltpu.VMEM)
SMEM = pl.BlockSpec(memory_space=pltpu.SMEM)


def limit(mib):
    return pltpu.CompilerParams(vmem_limit_bytes=mib << 20)


def call_prepare(count, queries, keys, values, cotangent, positions, cosine, phase, weight, frequencies, group, scale):
    rows = queries.shape[0]
    shapes = (
        ((WIDTH, rows), F32),
        ((WIDTH, rows), F32),
        ((HEADS, 2 * rows, 128), BF16),
        ((HEADS, 128, 2 * rows), BF16),
        ((HEADS, 128), F32),
        ((8 * group, rows), F32),
        ((8 * group, 128), F32),
        ((WIDTH, 192), BF16),
    )
    rows_of = [queries, keys, values, cotangent, positions]
    rows_of += [x.reshape(1, -1) for x in (cosine, phase, weight, frequencies)]
    return pl.pallas_call(
        functools.partial(prepare, rows, scale),
        name="prepare",
        grid=(1,),
        in_specs=[SMEM] + [pl.BlockSpec(x.shape, lambda i: (0, 0)) for x in rows_of],
        out_specs=[VMEM] * 8,
        out_shape=[jax.ShapeDtypeStruct(s, d) for s, d in shapes],
        scratch_shapes=[pltpu.VMEM((8, 128), F32), pltpu.VMEM((2 * NODES, WIDTH), F32)],
        compiler_params=limit(20),
    )(count, *rows_of)


def call_finish(count, mine, other):
    rows = mine[0].shape[1]
    return pl.pallas_call(
        functools.partial(finish, rows),
        name="finish",
        in_specs=[SMEM] + [VMEM] * 6,
        out_specs=[VMEM] * 3,
        out_shape=[jax.ShapeDtypeStruct((rows, WIDTH), BF16)] * 3,
        compiler_params=limit(16),
    )(count, *mine, *other)


def call_one(place, shards, proj, node, coef, qt, kt, w, tile=256):
    rows = proj.shape[1]
    group = proj.shape[0] // 8
    groups = len(shards)
    return pl.pallas_call(
        functools.partial(pass_one, rows, shards, group, tile),
        name="pass_one",
        in_specs=[SMEM] + [VMEM] * 6,
        out_specs=VMEM,
        out_shape=jax.ShapeDtypeStruct((groups * group, WIDTH, 128), F32),
        scratch_shapes=[
            pltpu.VMEM((group, 192, tile), BF16),
            pltpu.VMEM((HEADS, group * HD, 2 * tile), BF16),
            pltpu.VMEM((HEADS, group * HD, 2 * tile), BF16),
        ],
        compiler_params=limit(16),
    )(place, proj, node, coef, qt, kt, w)


def call_two(place, shards, proj, node, coef, kt, rhs, sg, grads, tile=256):
    rows = proj.shape[1]
    group = proj.shape[0] // 8
    groups = len(shards)
    out = jax.ShapeDtypeStruct((WIDTH, rows), F32)
    return pl.pallas_call(
        functools.partial(pass_two, rows, shards, group, tile),
        name="pass_two",
        in_specs=[SMEM] + [VMEM] * (6 + len(grads)),
        out_specs=[VMEM] * 3,
        out_shape=[out] * 3,
        scratch_shapes=[
            pltpu.VMEM((group, 192, tile), BF16),
            pltpu.VMEM((HEADS, group * HD, tile), BF16),
            pltpu.VMEM((groups, HEADS, HD, group * HD), BF16),
            pltpu.VMEM((group, WIDTH, tile), F32),
            pltpu.VMEM((group, WIDTH, tile), F32),
            pltpu.VMEM((HEADS, 2, group * HD, tile), F32),
            pltpu.VMEM((HEADS, 2, group * HD, tile), F32),
        ],
        input_output_aliases={7 + i: i for i in range(len(grads))},
        compiler_params=limit(20),
    )(place, proj, node, coef, kt, rhs, sg, *grads)


RING = (0, 2, 4, 6, 7, 5, 3, 1)
UP = tuple((RING[i], RING[(i + 1) % 8]) for i in range(8))
DOWN = tuple((b, a) for a, b in UP)
TOP = 60000.0


def send(up, down):
    return lax.ppermute(up, "atom", UP), lax.ppermute(down, "atom", DOWN)


def pack(part, bound):
    code = jnp.floor(jnp.log2(TOP / bound))
    n = part.shape[0]
    data = part.reshape(n, HEADS, HD, 128) * jnp.exp2(code)[None, :, None, :]
    rows = jnp.concatenate([data.reshape(n * WIDTH, 128), jnp.tile(code, (4, 1))], 0)
    return rows.astype(F16)


def unpack(got):
    code = got[-HEADS:].astype(F32)
    data = got[:-16].astype(F32).reshape(-1, HEADS, HD, 128)
    data = data * jnp.exp2(-code)[None, :, None, :]
    return data.reshape(-1, WIDTH, 128), TOP * jnp.exp2(-code)


def body(
    positions,
    queries,
    keys,
    values,
    cotangent,
    block_counts,
    dir_cos,
    dir_phase,
    dir_weight,
    frequencies,
):
    rows = queries.shape[0]
    n_atom = lax.axis_size("atom")
    scale = 1.0 / (8.0 * math.sqrt(rows * n_atom))
    local = dir_cos.shape[0]
    group = -(-local // 8)
    ringed = n_atom == 8
    node = jnp.asarray((_NODE.astype(np.float64) / (2 * np.pi)).astype(np.float32))[:, None]
    qt, kt, w, rhs, bound, proj, factor, coef = call_prepare(
        block_counts, queries, keys, values, cotangent, positions,
        dir_cos, dir_phase, dir_weight, frequencies, group, scale,
    )
    place = jnp.zeros((1,), jnp.int32)
    if ringed:
        block = lax.axis_index("atom").reshape(1)
        place = jnp.where(block % 2 == 0, block // 2, 7 - block // 2)

    def one(*shards, after=()):
        here, after = lax.optimization_barrier((place, after))
        return call_one(here, shards, proj, node, coef, qt, kt, w)

    def two(sg, shards, grads):
        return call_two(place, tuple(shards), proj, node, coef, kt, rhs, sg, grads)

    if ringed:
        half = group // 2
        part = one(4)
        ready = pack(part[:half], bound), pack(part[half:], bound)
        for ahead in (3, 2, 1):
            last = send(*ready)
            part = one(ahead, -ahead, after=ready)
            up, down = part[:group], part[group:]
            (got_up, up_bound), (got_down, down_bound) = unpack(last[0]), unpack(last[1])
            if ahead == 3:
                got_up = jnp.pad(got_up, ((0, group - half), (0, 0), (0, 0)))
                got_down = jnp.pad(got_down, ((half, 0), (0, 0), (0, 0)))
            ready = pack(up + got_up, bound + up_bound), pack(down + got_down, bound + down_bound)
        last = send(*ready)
        total = one(0, after=ready) + unpack(last[0])[0] + unpack(last[1])[0]
        own = lax.dynamic_slice_in_dim(factor, place[0] * group, group, 0)
        mine = (total * own[:, None, :]).astype(BF16)
        up, down = send(mine, mine)
        grads = two(mine, (0,), ())
        for ahead in (1, 2, 3):
            up, down, grads = lax.optimization_barrier((up, down, grads))
            both = jnp.concatenate([up, down], 0)
            if ahead < 3:
                up, down = send(up, down)
            else:
                up, down = send(up[:half], down[half:])
            grads = two(both, (-ahead, ahead), grads)
        grads = two(jnp.concatenate([up, down], 0), (4,), grads)
    else:
        part = one(*range(8)) * factor[:, None, :]
        grads = two(lax.psum(part, "atom").astype(BF16), range(8), ())
    other = [lax.ppermute(g, "dir", [(0, 1), (1, 0)]) for g in grads]
    return tuple(call_finish(block_counts, grads, other))


def solution(mesh):
    in_specs = (
        P(None, ("rep", "atom")),
        P(("rep", "atom"), None),
        P(("rep", "atom"), None),
        P(("rep", "atom"), None),
        P(("rep", "atom"), None),
        P(("rep", "atom")),
        P("dir"),
        P("dir"),
        P("dir"),
        P(),
    )
    out_specs = (P(("rep", "atom"), None), P(("rep", "atom"), None), P(("rep", "atom"), None))
    return jax.shard_map(body, mesh=mesh, in_specs=in_specs, out_specs=out_specs, check_vma=False)
```

```python
import functools
import math

import jax
import jax.numpy as jnp
import numpy as np
from jax import lax
from jax.experimental import pallas as pl
from jax.experimental.pallas import tpu as pltpu
from jax.sharding import PartitionSpec as P

HEADS = 4
HD = 64
HALF = 32
WIDTH = HEADS * HD
NODES = 16
F32 = jnp.float32
BF16 = jnp.bfloat16
F16 = jnp.float16

_NODE = np.cos((np.arange(NODES) + 0.5) * np.pi / (2 * NODES)).astype(np.float32)


def _fit(func, terms):
    z = 0.125 * (1 - np.cos((np.arange(256) + 0.5) * np.pi / 256))
    cheb = np.polynomial.chebyshev.Chebyshev.fit(z, func(z), terms - 1, domain=[0, 0.25])
    return [float(c) for c in cheb.convert(kind=np.polynomial.Polynomial).coef]


_SIN = _fit(lambda z: np.sin(2 * np.pi * np.sqrt(z)) / np.sqrt(z), 7)
_COS = _fit(lambda z: np.cos(2 * np.pi * np.sqrt(z)), 7)


def horner(coef, z):
    acc = coef[-1] * z + coef[-2]
    for c in coef[-3::-1]:
        acc = acc * z + c
    return acc


def store_coefs(coef_ref, full_ref, f):
    n64 = _NODE.astype(np.float64)
    nums = [(f - float(x)) * (f + float(x)) for x in _NODE]
    before, after = [None], [None]
    for i in range(NODES - 1):
        before.append(nums[i] if i == 0 else before[-1] * nums[i])
        k = NODES - 1 - i
        after.append(nums[k] if i == 0 else after[-1] * nums[k])
    after = after[::-1]
    full_ref[...] = jnp.zeros_like(full_ref)
    for j in range(NODES):
        den = np.delete(n64[j] ** 2 - n64**2, j)
        lead = before[j] if after[j] is None else after[j]
        if before[j] is not None and after[j] is not None:
            lead = before[j] * after[j]
        cosine = lead * float(1.0 / np.prod(den))
        full_ref[j : j + 1, :128] = cosine
        full_ref[NODES + j : NODES + j + 1, 128:] = cosine * (f * float(1.0 / n64[j]))
    full = full_ref[...]
    one = full.astype(BF16).astype(F32)
    two = (full - one).astype(BF16).astype(F32)
    three = full - one - two
    stacked = jnp.concatenate([one, two, three, one, two, one], 0)
    coef_ref[...] = jnp.transpose(stacked).astype(BF16)


def store_features(feat_ref, node_ref, proj_row):
    turns = node_ref[...] * proj_row
    turns = turns - jnp.round(turns)
    z = turns * turns
    full = jnp.concatenate([horner(_COS, z), turns * horner(_SIN, z)], axis=0)
    one = full.astype(BF16)
    rest = full - one.astype(F32)
    two = rest.astype(BF16)
    three = (rest - two.astype(F32)).astype(BF16)
    feat_ref[...] = jnp.concatenate([one, one, one, two, two, three], axis=0)


def prepare(rows, scale, count_ref, *refs):
    sources, outs, held, (table_ref, full_ref, sems) = refs[:9], refs[9:17], refs[17:26], refs[26:]
    copies = [
        pltpu.make_async_copy(src, dst, sems.at[i])
        for i, (src, dst) in enumerate(zip(sources, held))
    ]
    for copy in copies:
        copy.start()
    for copy in copies:
        copy.wait()
    prepared(rows, scale, count_ref, *held, *outs, table_ref, full_ref)


def prepared(rows, scale, count_ref, q_ref, k_ref, v_ref, d_ref, pos_ref, cos_ref, phase_ref, weight_ref, freq_ref, qt_ref, kt_ref, w_ref, rhs_ref, bound_ref, proj_ref, fac_ref, coef_ref, table_ref, full_ref):
    store_coefs(coef_ref, full_ref, freq_ref[...])
    local = cos_ref.shape[1]
    cosine, phase = cos_ref[...], phase_ref[...]
    sin_polar = jnp.sqrt(1.0 - cosine * cosine)
    table_ref[...] = jnp.zeros_like(table_ref)
    table_ref[0:1, :local] = sin_polar * jnp.cos(phase)
    table_ref[1:2, :local] = sin_polar * jnp.sin(phase)
    table_ref[2:3, :local] = cosine
    table_ref[3:4, :local] = scale * weight_ref[...]
    table = jnp.transpose(table_ref[...])[: proj_ref.shape[0]]
    proj_ref[...] = (
        table[:, 0:1] * pos_ref[0:1, :] + table[:, 1:2] * pos_ref[1:2, :] + table[:, 2:3] * pos_ref[2:3, :]
    )
    fac_ref[...] = jnp.broadcast_to(table[:, 3:4], fac_ref.shape)
    mask = (lax.broadcasted_iota(jnp.int32, (1, rows), 1) < count_ref[0]).astype(F32)
    lane = lax.broadcasted_iota(jnp.int32, (1, 128), 1)
    qt = jnp.transpose(q_ref[...].astype(F32)) * mask
    kt = jnp.transpose(k_ref[...].astype(F32)) * mask
    qt_ref[...] = qt
    kt_ref[...] = kt
    vt = jnp.transpose(v_ref[...].astype(F32))
    dt = jnp.transpose(d_ref[...].astype(F32))
    rhs_ref[...] = jnp.zeros_like(rhs_ref)
    zero = jnp.zeros((rows, HD), BF16)
    for h in range(HEADS):
        at = slice(h * HD, (h + 1) * HD)
        rhs_ref[h, :HD, :rows] = dt[at].astype(BF16)
        rhs_ref[h, HD:, rows:] = vt[at].astype(BF16)
        w_ref[h, :rows, :] = jnp.concatenate([v_ref[:, at], zero], 1)
        w_ref[h, rows:, :] = jnp.concatenate([zero, d_ref[:, at]], 1)

        def peak(x):
            most = jnp.max(jnp.abs(x[at]), axis=0, keepdims=True)
            return jnp.max(most, axis=1, keepdims=True)

        most = jnp.where(lane < HD, peak(kt) * peak(vt), peak(qt) * peak(dt))
        bound_ref[h : h + 1, :] = most * (1.5 * rows) + 1e-9


def finish(rows, count_ref, *refs):
    mask = (lax.broadcasted_iota(jnp.int32, (1, rows), 1) < count_ref[0]).astype(F32)
    for mine, other, out in zip(refs[:3], refs[3:6], refs[6:]):
        out[...] = jnp.transpose((mine[...] + other[...]) * mask).astype(BF16)


def shard_at(place_ref, shards, g):
    ahead = shards[-1] % 8
    for i in range(len(shards) - 2, -1, -1):
        ahead = jnp.where(g == i, shards[i] % 8, ahead)
    return lax.rem(place_ref[0] + ahead, 8)


def pass_one(rows, shards, group, tile, place_ref, proj_ref, node_ref, coef_ref, qt_ref, kt_ref, w_ref, rhs_ref, out_ref, qt_on, w_on, rhs_on, feat_ref, *rot_refs):
    per = rows // tile

    def one_group(g, unused):
        row = shard_at(place_ref, shards, g) * group

        def rotated(t):
            rot_ref = rot_refs[t % 2]
            at = slice(t * tile, (t + 1) * tile)
            for u in range(group):
                store_features(feat_ref.at[u], node_ref, proj_ref[pl.ds(row + u, 1), at])
            for u in range(group):
                trig = jnp.dot(coef_ref[...], feat_ref[u], preferred_element_type=F32)
                lo = slice(u * HD, u * HD + HALF)
                hi = slice(u * HD + HALF, (u + 1) * HD)
                for h in range(HEADS):
                    c = trig[h * HALF : (h + 1) * HALF]
                    s = trig[128 + h * HALF : 128 + (h + 1) * HALF]
                    for i, src in enumerate((kt_ref, qt_ref)):
                        to = slice(i * tile, (i + 1) * tile)
                        a = src[h * HD : h * HD + HALF, at]
                        b = src[h * HD + HALF : (h + 1) * HD, at]
                        rot_ref[h, lo, to] = (a * c - b * s).astype(BF16)
                        rot_ref[h, hi, to] = (a * s + b * c).astype(BF16)

        def summed(t):
            for h in range(HEADS):
                w = jnp.concatenate(
                    [w_ref[h, i * rows + t * tile : i * rows + (t + 1) * tile, :] for i in range(2)], 0
                )
                res = jnp.dot(rot_refs[t % 2][h], w, preferred_element_type=F32)
                for u in range(group):
                    part = res[u * HD : (u + 1) * HD]
                    if t == 0:
                        out_ref[g * group + u, h * HD : (h + 1) * HD, :] = part
                    else:
                        out_ref[g * group + u, h * HD : (h + 1) * HD, :] += part

        rotated(0)
        for t in range(1, per):
            rotated(t)
            summed(t - 1)
        summed(per - 1)
        return 0

    lax.fori_loop(0, len(shards), one_group, 0)


def pass_two(rows, shards, group, tile, place_ref, proj_ref, node_ref, coef_ref, kt_ref, rhs_ref, sg_ref, *rest):
    gq_ref, gk_ref, gv_ref, feat_ref, rot_ref, gst_ref, *pairs = rest[-10:]
    trig_refs, d_refs = pairs[:2], pairs[2:]
    if len(rest) == 13:
        gq_ref[...] = rest[0][...]
        gk_ref[...] = rest[1][...]
        gv_ref[...] = rest[2][...]
    else:
        gq_ref[...] = jnp.zeros_like(gq_ref)
        gk_ref[...] = jnp.zeros_like(gk_ref)
        gv_ref[...] = jnp.zeros_like(gv_ref)
    groups = len(shards)
    per = rows // tile
    total = groups * per

    def stacked(g, h):
        return jnp.concatenate(
            [sg_ref[g * group + u, h * HD : (h + 1) * HD, :] for u in range(group)], axis=0
        )

    for g in range(groups):
        for h in range(HEADS):
            gst_ref[g, h] = jnp.transpose(stacked(g, h)[:, HD:].astype(F32)).astype(BF16)

    def where(i):
        base = (i % per) * tile
        if not isinstance(i, int):
            base = pl.multiple_of(base, tile)
        return i // per, base

    def first(i, slot):
        g, base = where(i)
        row = shard_at(place_ref, shards, g) * group

        def trig(u):
            at = pl.ds(base, tile)
            store_features(feat_ref.at[u], node_ref, proj_ref[pl.ds(row + u, 1), at])
            trig_refs[slot][u] = jnp.dot(coef_ref[...], feat_ref[u], preferred_element_type=F32)

        def rotated(h, side):
            at = pl.ds(base + side * rows, tile)
            d_refs[slot][h, side] = jnp.dot(
                stacked(g, h), rhs_ref[h, :, at], preferred_element_type=F32
            )

        units = []
        for k in range(2 * HEADS):
            units.append([functools.partial(rotated, k // 2, k % 2)])
            if k < group:
                units[-1].append(functools.partial(trig, k))
        for u in range(2 * HEADS, group):
            units[-1].append(functools.partial(trig, u))
        return units

    def second(i, slot):
        g, base = where(i)
        at = pl.ds(base, tile)
        trig_ref, d_ref = trig_refs[slot], d_refs[slot]

        def head(h):
            lo = slice(h * HD, h * HD + HALF)
            hi = slice(h * HD + HALF, (h + 1) * HD)
            ka, kb = kt_ref[lo, at], kt_ref[hi, at]
            qa, qb, va, vb = gq_ref[lo, at], gq_ref[hi, at], gk_ref[lo, at], gk_ref[hi, at]
            for u in range(group):
                c = trig_ref[u, h * HALF : (h + 1) * HALF, :]
                s = trig_ref[u, 128 + h * HALF : 128 + (h + 1) * HALF, :]
                ulo = slice(u * HD, u * HD + HALF)
                uhi = slice(u * HD + HALF, (u + 1) * HD)
                rot_ref[h, ulo, :] = (ka * c - kb * s).astype(BF16)
                rot_ref[h, uhi, :] = (ka * s + kb * c).astype(BF16)
                a, b = d_ref[h, 0, ulo, :], d_ref[h, 0, uhi, :]
                qa, qb = qa + (a * c + b * s), qb + (b * c - a * s)
                a, b = d_ref[h, 1, ulo, :], d_ref[h, 1, uhi, :]
                va, vb = va + (a * c + b * s), vb + (b * c - a * s)
            gq_ref[lo, at], gq_ref[hi, at], gk_ref[lo, at], gk_ref[hi, at] = qa, qb, va, vb
            gv_ref[h * HD : (h + 1) * HD, at] += jnp.dot(
                gst_ref[g, h], rot_ref[h], preferred_element_type=F32
            )

        return [[functools.partial(head, k // 2)] if k % 2 else [] for k in range(2 * HEADS)]

    def run(*stages):
        for units in zip(*stages):
            for unit in units:
                for step in unit:
                    step()

    run(first(0, 0))

    def two_tiles(j, unused):
        run(first(2 * j + 1, 1), second(2 * j, 0))
        run(first(jnp.minimum(2 * j + 2, total - 1), 0), second(2 * j + 1, 1))
        return 0

    lax.fori_loop(0, total // 2, two_tiles, 0)


VMEM = pl.BlockSpec(memory_space=pltpu.VMEM)
SMEM = pl.BlockSpec(memory_space=pltpu.SMEM)


def limit(mib):
    return pltpu.CompilerParams(vmem_limit_bytes=mib << 20)


def call_prepare(count, queries, keys, values, cotangent, positions, cosine, phase, weight, frequencies, group, scale):
    rows = queries.shape[0]
    shapes = (
        ((WIDTH, rows), F32),
        ((WIDTH, rows), F32),
        ((HEADS, 2 * rows, 128), BF16),
        ((HEADS, 128, 2 * rows), BF16),
        ((HEADS, 128), F32),
        ((8 * group, rows), F32),
        ((8 * group, 128), F32),
        ((WIDTH, 192), BF16),
    )
    rows_of = [queries, keys, values, cotangent, positions]
    rows_of += [x.reshape(1, -1) for x in (cosine, phase, weight, frequencies)]
    return pl.pallas_call(
        functools.partial(prepare, rows, scale),
        name="prepare",
        in_specs=[SMEM] + [pl.BlockSpec(memory_space=pltpu.HBM)] * len(rows_of),
        out_specs=[VMEM] * 8,
        out_shape=[jax.ShapeDtypeStruct(s, d) for s, d in shapes],
        scratch_shapes=[pltpu.VMEM(x.shape, x.dtype) for x in rows_of]
        + [
            pltpu.VMEM((8, 128), F32),
            pltpu.VMEM((2 * NODES, WIDTH), F32),
            pltpu.SemaphoreType.DMA((len(rows_of),)),
        ],
        compiler_params=limit(20),
    )(count, *[pltpu.with_memory_space_constraint(x, pltpu.HBM) for x in rows_of])


def call_finish(count, mine, other):
    rows = mine[0].shape[1]
    return pl.pallas_call(
        functools.partial(finish, rows),
        name="finish",
        in_specs=[SMEM] + [VMEM] * 6,
        out_specs=[VMEM] * 3,
        out_shape=[jax.ShapeDtypeStruct((rows, WIDTH), BF16)] * 3,
        compiler_params=limit(16),
    )(count, *mine, *other)


def call_one(place, shards, proj, node, coef, qt, kt, w, rhs, tile=256):
    rows = proj.shape[1]
    group = proj.shape[0] // 8
    groups = len(shards)
    return pl.pallas_call(
        functools.partial(pass_one, rows, shards, group, tile),
        name="pass_one",
        in_specs=[SMEM] + [VMEM] * 7,
        out_specs=[VMEM] * 4,
        out_shape=[
            jax.ShapeDtypeStruct((groups * group, WIDTH, 128), F32),
            jax.ShapeDtypeStruct(qt.shape, qt.dtype),
            jax.ShapeDtypeStruct(w.shape, w.dtype),
            jax.ShapeDtypeStruct(rhs.shape, rhs.dtype),
        ],
        input_output_aliases={4: 1, 6: 2, 7: 3},
        scratch_shapes=[
            pltpu.VMEM((group, 192, tile), BF16),
            pltpu.VMEM((HEADS, group * HD, 2 * tile), BF16),
            pltpu.VMEM((HEADS, group * HD, 2 * tile), BF16),
        ],
        compiler_params=limit(16),
    )(place, proj, node, coef, qt, kt, w, rhs)


def call_two(place, shards, proj, node, coef, kt, rhs, sg, grads, tile=256):
    rows = proj.shape[1]
    group = proj.shape[0] // 8
    groups = len(shards)
    out = jax.ShapeDtypeStruct((WIDTH, rows), F32)
    return pl.pallas_call(
        functools.partial(pass_two, rows, shards, group, tile),
        name="pass_two",
        in_specs=[SMEM] + [VMEM] * (6 + len(grads)),
        out_specs=[VMEM] * 3,
        out_shape=[out] * 3,
        scratch_shapes=[
            pltpu.VMEM((group, 192, tile), BF16),
            pltpu.VMEM((HEADS, group * HD, tile), BF16),
            pltpu.VMEM((groups, HEADS, HD, group * HD), BF16),
            pltpu.VMEM((group, WIDTH, tile), F32),
            pltpu.VMEM((group, WIDTH, tile), F32),
            pltpu.VMEM((HEADS, 2, group * HD, tile), F32),
            pltpu.VMEM((HEADS, 2, group * HD, tile), F32),
        ],
        input_output_aliases={7 + i: i for i in range(len(grads))},
        compiler_params=limit(20),
    )(place, proj, node, coef, kt, rhs, sg, *grads)


RING = (0, 2, 4, 6, 7, 5, 3, 1)
UP = tuple((RING[i], RING[(i + 1) % 8]) for i in range(8))
DOWN = tuple((b, a) for a, b in UP)
TOP = 60000.0


def send(up, down):
    return lax.ppermute(up, "atom", UP), lax.ppermute(down, "atom", DOWN)


def pack(part, bound):
    code = jnp.floor(jnp.log2(TOP / bound))
    n = part.shape[0]
    data = part.reshape(n, HEADS, HD, 128) * jnp.exp2(code)[None, :, None, :]
    rows = jnp.concatenate([data.reshape(n * WIDTH, 128), jnp.tile(code, (4, 1))], 0)
    return rows.astype(F16)


def unpack(got):
    code = got[-HEADS:].astype(F32)
    data = got[:-16].astype(F32).reshape(-1, HEADS, HD, 128)
    data = data * jnp.exp2(-code)[None, :, None, :]
    return data.reshape(-1, WIDTH, 128), TOP * jnp.exp2(-code)


def body(
    positions,
    queries,
    keys,
    values,
    cotangent,
    block_counts,
    dir_cos,
    dir_phase,
    dir_weight,
    frequencies,
):
    rows = queries.shape[0]
    n_atom = lax.axis_size("atom")
    scale = 1.0 / (8.0 * math.sqrt(rows * n_atom))
    local = dir_cos.shape[0]
    group = -(-local // 8)
    ringed = n_atom == 8
    node = jnp.asarray((_NODE.astype(np.float64) / (2 * np.pi)).astype(np.float32))[:, None]
    qt, kt, w, rhs, bound, proj, factor, coef = call_prepare(
        block_counts, queries, keys, values, cotangent, positions,
        dir_cos, dir_phase, dir_weight, frequencies, group, scale,
    )
    place = jnp.zeros((1,), jnp.int32)
    if ringed:
        block = lax.axis_index("atom").reshape(1)
        place = jnp.where(block % 2 == 0, block // 2, 7 - block // 2)

    held = [qt, w, rhs]

    def one(*shards, after=()):
        here, after = lax.optimization_barrier((place, after))
        part, *held[:] = call_one(here, shards, proj, node, coef, held[0], kt, *held[1:])
        return part

    def two(sg, shards, grads):
        return call_two(place, tuple(shards), proj, node, coef, kt, held[2], sg, grads)

    if ringed:
        half = group // 2
        part = one(4)
        ready = pack(part[:half], bound), pack(part[half:], bound)
        for ahead in (3, 2, 1):
            last = send(*ready)
            part = one(ahead, -ahead, after=ready)
            up, down = part[:group], part[group:]
            (got_up, up_bound), (got_down, down_bound) = unpack(last[0]), unpack(last[1])
            if ahead == 3:
                got_up = jnp.pad(got_up, ((0, group - half), (0, 0), (0, 0)))
                got_down = jnp.pad(got_down, ((half, 0), (0, 0), (0, 0)))
            ready = pack(up + got_up, bound + up_bound), pack(down + got_down, bound + down_bound)
        last = send(*ready)
        total = one(0, after=ready) + unpack(last[0])[0] + unpack(last[1])[0]
        own = lax.dynamic_slice_in_dim(factor, place[0] * group, group, 0)
        mine = (total * own[:, None, :]).astype(BF16)
        up, down = send(mine, mine)
        grads = two(mine, (0,), ())
        for ahead in (1, 2, 3):
            up, down, grads = lax.optimization_barrier((up, down, grads))
            both = jnp.concatenate([up, down], 0)
            if ahead < 3:
                up, down = send(up, down)
            else:
                up, down = send(up[:half], down[half:])
            grads = two(both, (-ahead, ahead), grads)
        grads = two(jnp.concatenate([up, down], 0), (4,), grads)
    else:
        part = one(*range(8)) * factor[:, None, :]
        grads = two(lax.psum(part, "atom").astype(BF16), range(8), ())
    other = [lax.ppermute(g, "dir", [(0, 1), (1, 0)]) for g in grads]
    return tuple(call_finish(block_counts, grads, other))


def solution(mesh):
    in_specs = (
        P(None, ("rep", "atom")),
        P(("rep", "atom"), None),
        P(("rep", "atom"), None),
        P(("rep", "atom"), None),
        P(("rep", "atom"), None),
        P(("rep", "atom")),
        P("dir"),
        P("dir"),
        P("dir"),
        P(),
    )
    out_specs = (P(("rep", "atom"), None), P(("rep", "atom"), None), P(("rep", "atom"), None))
    return jax.shard_map(body, mesh=mesh, in_specs=in_specs, out_specs=out_specs, check_vma=False)
```

```python
import functools
import math

import jax
import jax.numpy as jnp
import numpy as np
from jax import lax
from jax.experimental import pallas as pl
from jax.experimental.pallas import tpu as pltpu
from jax.sharding import PartitionSpec as P

HEADS = 4
HD = 64
HALF = 32
WIDTH = HEADS * HD
NODES = 16
F32 = jnp.float32
BF16 = jnp.bfloat16
F16 = jnp.float16

_NODE = np.cos((np.arange(NODES) + 0.5) * np.pi / (2 * NODES)).astype(np.float32)


def _fit(func, terms):
    z = 0.125 * (1 - np.cos((np.arange(256) + 0.5) * np.pi / 256))
    cheb = np.polynomial.chebyshev.Chebyshev.fit(z, func(z), terms - 1, domain=[0, 0.25])
    return [float(c) for c in cheb.convert(kind=np.polynomial.Polynomial).coef]


_SIN = _fit(lambda z: np.sin(2 * np.pi * np.sqrt(z)) / np.sqrt(z), 7)
_COS = _fit(lambda z: np.cos(2 * np.pi * np.sqrt(z)), 7)


def horner(coef, z):
    acc = coef[-1] * z + coef[-2]
    for c in coef[-3::-1]:
        acc = acc * z + c
    return acc


def store_coefs(coef_ref, full_ref, f):
    n64 = _NODE.astype(np.float64)
    nums = [(f - float(x)) * (f + float(x)) for x in _NODE]
    before, after = [None], [None]
    for i in range(NODES - 1):
        before.append(nums[i] if i == 0 else before[-1] * nums[i])
        k = NODES - 1 - i
        after.append(nums[k] if i == 0 else after[-1] * nums[k])
    after = after[::-1]
    full_ref[...] = jnp.zeros_like(full_ref)
    for j in range(NODES):
        den = np.delete(n64[j] ** 2 - n64**2, j)
        lead = before[j] if after[j] is None else after[j]
        if before[j] is not None and after[j] is not None:
            lead = before[j] * after[j]
        cosine = lead * float(1.0 / np.prod(den))
        full_ref[j : j + 1, :128] = cosine
        full_ref[NODES + j : NODES + j + 1, 128:] = cosine * (f * float(1.0 / n64[j]))
    full = full_ref[...]
    one = full.astype(BF16).astype(F32)
    two = (full - one).astype(BF16).astype(F32)
    three = full - one - two
    stacked = jnp.concatenate([one, two, three, one, two, one], 0)
    coef_ref[...] = jnp.transpose(stacked).astype(BF16)


def store_features(feat_ref, node_ref, proj_row):
    turns = node_ref[...] * proj_row
    turns = turns - jnp.round(turns)
    z = turns * turns
    full = jnp.concatenate([horner(_COS, z), turns * horner(_SIN, z)], axis=0)
    one = full.astype(BF16)
    rest = full - one.astype(F32)
    two = rest.astype(BF16)
    three = (rest - two.astype(F32)).astype(BF16)
    feat_ref[...] = jnp.concatenate([one, one, one, two, two, three], axis=0)


def prepare(rows, scale, count_ref, *refs):
    sources, outs, held, (table_ref, full_ref, sems) = refs[:9], refs[9:17], refs[17:26], refs[26:]
    copies = [
        pltpu.make_async_copy(src, dst, sems.at[i])
        for i, (src, dst) in enumerate(zip(sources, held))
    ]
    for copy in copies:
        copy.start()
    for copy in copies:
        copy.wait()
    prepared(rows, scale, count_ref, *held, *outs, table_ref, full_ref)


def prepared(rows, scale, count_ref, q_ref, k_ref, v_ref, d_ref, pos_ref, cos_ref, phase_ref, weight_ref, freq_ref, qt_ref, kt_ref, w_ref, rhs_ref, bound_ref, proj_ref, fac_ref, coef_ref, table_ref, full_ref):
    store_coefs(coef_ref, full_ref, freq_ref[...])
    local = cos_ref.shape[1]
    cosine, phase = cos_ref[...], phase_ref[...]
    sin_polar = jnp.sqrt(1.0 - cosine * cosine)
    table_ref[...] = jnp.zeros_like(table_ref)
    table_ref[0:1, :local] = sin_polar * jnp.cos(phase)
    table_ref[1:2, :local] = sin_polar * jnp.sin(phase)
    table_ref[2:3, :local] = cosine
    table_ref[3:4, :local] = scale * weight_ref[...]
    table = jnp.transpose(table_ref[...])[: proj_ref.shape[0]]
    proj_ref[...] = (
        table[:, 0:1] * pos_ref[0:1, :] + table[:, 1:2] * pos_ref[1:2, :] + table[:, 2:3] * pos_ref[2:3, :]
    )
    fac_ref[...] = jnp.broadcast_to(table[:, 3:4], fac_ref.shape)
    mask = (lax.broadcasted_iota(jnp.int32, (1, rows), 1) < count_ref[0]).astype(F32)
    lane = lax.broadcasted_iota(jnp.int32, (1, 128), 1)
    qt = jnp.transpose(q_ref[...].astype(F32)) * mask
    kt = jnp.transpose(k_ref[...].astype(F32)) * mask
    qt_ref[...] = qt
    kt_ref[...] = kt
    vt = jnp.transpose(v_ref[...].astype(F32))
    dt = jnp.transpose(d_ref[...].astype(F32))
    rhs_ref[...] = jnp.zeros_like(rhs_ref)
    zero = jnp.zeros((rows, HD), BF16)
    for h in range(HEADS):
        at = slice(h * HD, (h + 1) * HD)
        rhs_ref[h, :HD, :rows] = dt[at].astype(BF16)
        rhs_ref[h, HD:, rows:] = vt[at].astype(BF16)
        w_ref[h, :rows, :] = jnp.concatenate([v_ref[:, at], zero], 1)
        w_ref[h, rows:, :] = jnp.concatenate([zero, d_ref[:, at]], 1)

        def peak(x):
            most = jnp.max(jnp.abs(x[at]), axis=0, keepdims=True)
            return jnp.max(most, axis=1, keepdims=True)

        most = jnp.where(lane < HD, peak(kt) * peak(vt), peak(qt) * peak(dt))
        bound_ref[h : h + 1, :] = most * (1.5 * rows) + 1e-9


def finish(rows, count_ref, *refs):
    mask = (lax.broadcasted_iota(jnp.int32, (1, rows), 1) < count_ref[0]).astype(F32)
    for mine, other, out in zip(refs[:3], refs[3:6], refs[6:]):
        out[...] = jnp.transpose((mine[...] + other[...]) * mask).astype(BF16)


def shard_at(place_ref, shards, g):
    ahead = shards[-1] % 8
    for i in range(len(shards) - 2, -1, -1):
        ahead = jnp.where(g == i, shards[i] % 8, ahead)
    return lax.rem(place_ref[0] + ahead, 8)


def pass_one(rows, shards, group, tile, place_ref, proj_ref, node_ref, coef_ref, qt_ref, kt_ref, w_ref, rhs_ref, out_ref, qt_on, w_on, rhs_on, feat_ref, *rot_refs):
    per = rows // tile

    def one_group(g, unused):
        row = shard_at(place_ref, shards, g) * group

        def rotated(t):
            rot_ref = rot_refs[t % 2]
            at = slice(t * tile, (t + 1) * tile)
            for u in range(group):
                store_features(feat_ref.at[u], node_ref, proj_ref[pl.ds(row + u, 1), at])
            for u in range(group):
                trig = jnp.dot(coef_ref[...], feat_ref[u], preferred_element_type=F32)
                lo = slice(u * HD, u * HD + HALF)
                hi = slice(u * HD + HALF, (u + 1) * HD)
                for h in range(HEADS):
                    c = trig[h * HALF : (h + 1) * HALF]
                    s = trig[128 + h * HALF : 128 + (h + 1) * HALF]
                    for i, src in enumerate((kt_ref, qt_ref)):
                        to = slice(i * tile, (i + 1) * tile)
                        a = src[h * HD : h * HD + HALF, at]
                        b = src[h * HD + HALF : (h + 1) * HD, at]
                        rot_ref[h, lo, to] = (a * c - b * s).astype(BF16)
                        rot_ref[h, hi, to] = (a * s + b * c).astype(BF16)

        def summed(t):
            for h in range(HEADS):
                w = jnp.concatenate(
                    [w_ref[h, i * rows + t * tile : i * rows + (t + 1) * tile, :] for i in range(2)], 0
                )
                res = jnp.dot(rot_refs[t % 2][h], w, preferred_element_type=F32)
                for u in range(group):
                    part = res[u * HD : (u + 1) * HD]
                    if t == 0:
                        out_ref[g * group + u, h * HD : (h + 1) * HD, :] = part
                    else:
                        out_ref[g * group + u, h * HD : (h + 1) * HD, :] += part

        rotated(0)
        for t in range(1, per):
            rotated(t)
            summed(t - 1)
        summed(per - 1)
        return 0

    lax.fori_loop(0, len(shards), one_group, 0)


def pass_two(rows, shards, group, tile, place_ref, proj_ref, node_ref, coef_ref, kt_ref, rhs_ref, sg_ref, *rest):
    gq_ref, gk_ref, gv_ref, feat_ref, rot_ref, gst_ref, *pairs = rest[-10:]
    trig_refs, d_refs = pairs[:2], pairs[2:]
    if len(rest) == 13:
        gq_ref[...] = rest[0][...]
        gk_ref[...] = rest[1][...]
        gv_ref[...] = rest[2][...]
    else:
        gq_ref[...] = jnp.zeros_like(gq_ref)
        gk_ref[...] = jnp.zeros_like(gk_ref)
        gv_ref[...] = jnp.zeros_like(gv_ref)
    groups = len(shards)
    per = rows // tile
    total = groups * per

    def stacked(g, h):
        return jnp.concatenate(
            [sg_ref[g * group + u, h * HD : (h + 1) * HD, :] for u in range(group)], axis=0
        )

    for g in range(groups):
        for h in range(HEADS):
            gst_ref[g, h] = jnp.transpose(stacked(g, h)[:, HD:].astype(F32)).astype(BF16)

    def where(i):
        base = (i % per) * tile
        if not isinstance(i, int):
            base = pl.multiple_of(base, tile)
        return i // per, base

    def first(i, slot):
        g, base = where(i)
        row = shard_at(place_ref, shards, g) * group

        def trig(u):
            at = pl.ds(base, tile)
            store_features(feat_ref.at[u], node_ref, proj_ref[pl.ds(row + u, 1), at])
            trig_refs[slot][u] = jnp.dot(coef_ref[...], feat_ref[u], preferred_element_type=F32)

        def rotated(h, side):
            at = pl.ds(base + side * rows, tile)
            d_refs[slot][h, side] = jnp.dot(
                stacked(g, h), rhs_ref[h, :, at], preferred_element_type=F32
            )

        units = []
        for k in range(2 * HEADS):
            units.append([functools.partial(rotated, k // 2, k % 2)])
            if k < group:
                units[-1].append(functools.partial(trig, k))
        for u in range(2 * HEADS, group):
            units[-1].append(functools.partial(trig, u))
        return units

    def second(i, slot):
        g, base = where(i)
        at = pl.ds(base, tile)
        trig_ref, d_ref = trig_refs[slot], d_refs[slot]

        def head(h):
            lo = slice(h * HD, h * HD + HALF)
            hi = slice(h * HD + HALF, (h + 1) * HD)
            ka, kb = kt_ref[lo, at], kt_ref[hi, at]
            qa, qb, va, vb = gq_ref[lo, at], gq_ref[hi, at], gk_ref[lo, at], gk_ref[hi, at]
            for u in range(group):
                c = trig_ref[u, h * HALF : (h + 1) * HALF, :]
                s = trig_ref[u, 128 + h * HALF : 128 + (h + 1) * HALF, :]
                ulo = slice(u * HD, u * HD + HALF)
                uhi = slice(u * HD + HALF, (u + 1) * HD)
                rot_ref[h, ulo, :] = (ka * c - kb * s).astype(BF16)
                rot_ref[h, uhi, :] = (ka * s + kb * c).astype(BF16)
                a, b = d_ref[h, 0, ulo, :], d_ref[h, 0, uhi, :]
                qa, qb = qa + (a * c + b * s), qb + (b * c - a * s)
                a, b = d_ref[h, 1, ulo, :], d_ref[h, 1, uhi, :]
                va, vb = va + (a * c + b * s), vb + (b * c - a * s)
            gq_ref[lo, at], gq_ref[hi, at], gk_ref[lo, at], gk_ref[hi, at] = qa, qb, va, vb
            gv_ref[h * HD : (h + 1) * HD, at] += jnp.dot(
                gst_ref[g, h], rot_ref[h], preferred_element_type=F32
            )

        return [[functools.partial(head, k // 2)] if k % 2 else [] for k in range(2 * HEADS)]

    def run(*stages):
        for units in zip(*stages):
            for unit in units:
                for step in unit:
                    step()

    run(first(0, 0))

    def two_tiles(j, unused):
        run(first(2 * j + 1, 1), second(2 * j, 0))
        run(first(jnp.minimum(2 * j + 2, total - 1), 0), second(2 * j + 1, 1))
        return 0

    if groups > 1:
        lax.fori_loop(0, total // 2, two_tiles, 0)
    else:
        lax.fori_loop(0, total // 2 - 1, two_tiles, 0)
        run(first(total - 1, 1), second(total - 2, 0))
        run(second(total - 1, 1))


VMEM = pl.BlockSpec(memory_space=pltpu.VMEM)
SMEM = pl.BlockSpec(memory_space=pltpu.SMEM)


def limit(mib):
    return pltpu.CompilerParams(vmem_limit_bytes=mib << 20)


def call_prepare(count, queries, keys, values, cotangent, positions, cosine, phase, weight, frequencies, group, scale):
    rows = queries.shape[0]
    shapes = (
        ((WIDTH, rows), F32),
        ((WIDTH, rows), F32),
        ((HEADS, 2 * rows, 128), BF16),
        ((HEADS, 128, 2 * rows), BF16),
        ((HEADS, 128), F32),
        ((8 * group, rows), F32),
        ((8 * group, 128), F32),
        ((WIDTH, 192), BF16),
    )
    rows_of = [queries, keys, values, cotangent, positions]
    rows_of += [x.reshape(1, -1) for x in (cosine, phase, weight, frequencies)]
    return pl.pallas_call(
        functools.partial(prepare, rows, scale),
        name="prepare",
        in_specs=[SMEM] + [pl.BlockSpec(memory_space=pltpu.HBM)] * len(rows_of),
        out_specs=[VMEM] * 8,
        out_shape=[jax.ShapeDtypeStruct(s, d) for s, d in shapes],
        scratch_shapes=[pltpu.VMEM(x.shape, x.dtype) for x in rows_of]
        + [
            pltpu.VMEM((8, 128), F32),
            pltpu.VMEM((2 * NODES, WIDTH), F32),
            pltpu.SemaphoreType.DMA((len(rows_of),)),
        ],
        compiler_params=limit(20),
    )(count, *[pltpu.with_memory_space_constraint(x, pltpu.HBM) for x in rows_of])


def call_finish(count, mine, other):
    rows = mine[0].shape[1]
    return pl.pallas_call(
        functools.partial(finish, rows),
        name="finish",
        in_specs=[SMEM] + [VMEM] * 6,
        out_specs=[VMEM] * 3,
        out_shape=[jax.ShapeDtypeStruct((rows, WIDTH), BF16)] * 3,
        compiler_params=limit(16),
    )(count, *mine, *other)


def call_one(place, shards, proj, node, coef, qt, kt, w, rhs, tile=256):
    rows = proj.shape[1]
    group = proj.shape[0] // 8
    groups = len(shards)
    return pl.pallas_call(
        functools.partial(pass_one, rows, shards, group, tile),
        name="pass_one",
        in_specs=[SMEM] + [VMEM] * 7,
        out_specs=[VMEM] * 4,
        out_shape=[
            jax.ShapeDtypeStruct((groups * group, WIDTH, 128), F32),
            jax.ShapeDtypeStruct(qt.shape, qt.dtype),
            jax.ShapeDtypeStruct(w.shape, w.dtype),
            jax.ShapeDtypeStruct(rhs.shape, rhs.dtype),
        ],
        input_output_aliases={4: 1, 6: 2, 7: 3},
        scratch_shapes=[
            pltpu.VMEM((group, 192, tile), BF16),
            pltpu.VMEM((HEADS, group * HD, 2 * tile), BF16),
            pltpu.VMEM((HEADS, group * HD, 2 * tile), BF16),
        ],
        compiler_params=limit(16),
    )(place, proj, node, coef, qt, kt, w, rhs)


def call_two(place, shards, proj, node, coef, kt, rhs, sg, grads, tile=256):
    rows = proj.shape[1]
    group = proj.shape[0] // 8
    groups = len(shards)
    out = jax.ShapeDtypeStruct((WIDTH, rows), F32)
    return pl.pallas_call(
        functools.partial(pass_two, rows, shards, group, tile),
        name="pass_two",
        in_specs=[SMEM] + [VMEM] * (6 + len(grads)),
        out_specs=[VMEM] * 3,
        out_shape=[out] * 3,
        scratch_shapes=[
            pltpu.VMEM((group, 192, tile), BF16),
            pltpu.VMEM((HEADS, group * HD, tile), BF16),
            pltpu.VMEM((groups, HEADS, HD, group * HD), BF16),
            pltpu.VMEM((group, WIDTH, tile), F32),
            pltpu.VMEM((group, WIDTH, tile), F32),
            pltpu.VMEM((HEADS, 2, group * HD, tile), F32),
            pltpu.VMEM((HEADS, 2, group * HD, tile), F32),
        ],
        input_output_aliases={7 + i: i for i in range(len(grads))},
        compiler_params=limit(20),
    )(place, proj, node, coef, kt, rhs, sg, *grads)


RING = (0, 2, 4, 6, 7, 5, 3, 1)
UP = tuple((RING[i], RING[(i + 1) % 8]) for i in range(8))
DOWN = tuple((b, a) for a, b in UP)
TOP = 60000.0


def send(up, down):
    return lax.ppermute(up, "atom", UP), lax.ppermute(down, "atom", DOWN)


def pack(part, bound):
    code = jnp.floor(jnp.log2(TOP / bound))
    n = part.shape[0]
    data = part.reshape(n, HEADS, HD, 128) * jnp.exp2(code)[None, :, None, :]
    rows = jnp.concatenate([data.reshape(n * WIDTH, 128), jnp.tile(code, (4, 1))], 0)
    return rows.astype(F16)


def unpack(got):
    code = got[-HEADS:].astype(F32)
    data = got[:-16].astype(F32).reshape(-1, HEADS, HD, 128)
    data = data * jnp.exp2(-code)[None, :, None, :]
    return data.reshape(-1, WIDTH, 128), TOP * jnp.exp2(-code)


def body(
    positions,
    queries,
    keys,
    values,
    cotangent,
    block_counts,
    dir_cos,
    dir_phase,
    dir_weight,
    frequencies,
):
    rows = queries.shape[0]
    n_atom = lax.axis_size("atom")
    scale = 1.0 / (8.0 * math.sqrt(rows * n_atom))
    local = dir_cos.shape[0]
    group = -(-local // 8)
    ringed = n_atom == 8
    node = jnp.asarray((_NODE.astype(np.float64) / (2 * np.pi)).astype(np.float32))[:, None]
    qt, kt, w, rhs, bound, proj, factor, coef = call_prepare(
        block_counts, queries, keys, values, cotangent, positions,
        dir_cos, dir_phase, dir_weight, frequencies, group, scale,
    )
    place = jnp.zeros((1,), jnp.int32)
    if ringed:
        block = lax.axis_index("atom").reshape(1)
        place = jnp.where(block % 2 == 0, block // 2, 7 - block // 2)

    held = [qt, w, rhs]

    def one(*shards, after=()):
        here, after = lax.optimization_barrier((place, after))
        part, *held[:] = call_one(here, shards, proj, node, coef, held[0], kt, *held[1:])
        return part

    def two(sg, shards, grads):
        return call_two(place, tuple(shards), proj, node, coef, kt, held[2], sg, grads)

    if ringed:
        half = group // 2
        part = one(4)
        ready = pack(part[:half], bound), pack(part[half:], bound)
        for ahead in (3, 2, 1):
            last = send(*ready)
            part = one(ahead, -ahead, after=ready)
            up, down = part[:group], part[group:]
            (got_up, up_bound), (got_down, down_bound) = unpack(last[0]), unpack(last[1])
            if ahead == 3:
                got_up = jnp.pad(got_up, ((0, group - half), (0, 0), (0, 0)))
                got_down = jnp.pad(got_down, ((half, 0), (0, 0), (0, 0)))
            ready = pack(up + got_up, bound + up_bound), pack(down + got_down, bound + down_bound)
        last = send(*ready)
        total = one(0, after=ready) + unpack(last[0])[0] + unpack(last[1])[0]
        own = lax.dynamic_slice_in_dim(factor, place[0] * group, group, 0)
        mine = (total * own[:, None, :]).astype(BF16)
        up, down = send(mine, mine)
        grads = two(mine, (0,), ())
        for ahead in (1, 2, 3):
            up, down, grads = lax.optimization_barrier((up, down, grads))
            both = jnp.concatenate([up, down], 0)
            if ahead < 3:
                up, down = send(up, down)
            else:
                up, down = send(up[:half], down[half:])
            grads = two(both, (-ahead, ahead), grads)
        grads = two(jnp.concatenate([up, down], 0), (4,), grads)
    else:
        part = one(*range(8)) * factor[:, None, :]
        grads = two(lax.psum(part, "atom").astype(BF16), range(8), ())
    other = [lax.ppermute(g, "dir", [(0, 1), (1, 0)]) for g in grads]
    return tuple(call_finish(block_counts, grads, other))


def solution(mesh):
    in_specs = (
        P(None, ("rep", "atom")),
        P(("rep", "atom"), None),
        P(("rep", "atom"), None),
        P(("rep", "atom"), None),
        P(("rep", "atom"), None),
        P(("rep", "atom")),
        P("dir"),
        P("dir"),
        P("dir"),
        P(),
    )
    out_specs = (P(("rep", "atom"), None), P(("rep", "atom"), None), P(("rep", "atom"), None))
    return jax.shard_map(body, mesh=mesh, in_specs=in_specs, out_specs=out_specs, check_vma=False)
```
